1024 devices in a mesh: row: 32 (over y, z_lo), col: 32 (over x, z_hi, core).
Axes of the slice: x: 8, y: 8, z: 8 (z_hi: 2, z_lo: 4; z = z_hi * 4 + z_lo), core: 2. Of those that a mesh axis runs over, the one named last changes fastest.
Arguments:
- spectra: bfloat16 [600, 128, 4096], P(None, 'row', 'col'), may hold values from 0.0099487305 to 1
- wind: float32 [2, 128, 4096], P(None, 'row', 'col'), may hold values from -18 to 18
- wave_current: float32 [3, 128, 4096], P(None, 'row', 'col'), may hold values from -3 to 3
- wave_wet: int32 [128, 4096], P('row', 'col'), may hold values 0 or 1
- interaction: bfloat16 [600, 600], replicated, may hold values from -0.25 to 0.25
- input_rate: float32 [25], replicated, may hold values from 0.002 to 0.03
- eta_gain: float32 [25], replicated, may hold values from -0.5 to 0.5
- stress_map: float32 [2, 600], replicated, may hold values from -0.25 to 0.25
- stokes_map: float32 [6, 600], replicated, may hold values from -0.25 to 0.25
- ocean_vel: float32 [2, 30, 256, 4096], P(None, None, 'row', 'col'), may hold values from -3 to 3
- ocean_eta: float32 [256, 4096], P('row', 'col'), may hold values from -3 to 3
- ocean_wet: int32 [256, 4096], P('row', 'col'), may hold values 0 or 1
- coriolis: float32 [256, 4096], P('row', 'col'), may hold values from -1.5 to 1.5
- tau_profile: float32 [30], replicated, may hold values from 0.05 to 1
- stokes_profile: float32 [3, 30], replicated, may hold values from 0.05 to 1
- thickness: float32 [30], replicated, may hold values from 0.02 to 0.1
- mix_inverse: float32 [30, 30], replicated
- fold_index: int32 [4096], P('col'), may hold values from 0 to 4095, as said below
- wave_send: int32 [32, 32, 3, 64], P('row', 'col'), may hold values from 0 to 511
- ocean_recv: bfloat16 [32, 32, 3, 64, 1024], P('row', 'col'), may hold values from -0.4375 to 0.4375
- ocean_send: int32 [32, 32, 3, 64], P('row', 'col'), may hold values from 0 to 1023
- wave_recv: bfloat16 [32, 32, 3, 64, 512], P('row', 'col'), may hold values from -0.4375 to 0.4375
Outputs:
- spectra_out: bfloat16 [600, 128, 4096], P(None, 'row', 'col')
- ocean_vel_out: float32 [2, 30, 256, 4096], P(None, None, 'row', 'col')
- ocean_eta_out: float32 [256, 4096], P('row', 'col')
- current_out: float32 [3, 128, 4096], P(None, 'row', 'col')
The draws below stay inside these ranges and needn't reach their ends.
Inputs may be any that keep to these rules, and one draw needn't show every extreme that they name: `wave_send`: entries name cells of the sending wave tile numbered y * 128 + x. `ocean_send`: entries name cells of the sending ocean tile numbered y * 128 + x. `fold_index`: each entry names a column of the whole top line; columns of any block may be named from any block.
All inputs are finite; a program needn't handle non-finite values. No bound on the sum of `wave_wet` or of `ocean_wet` on one device may be relied on, other than what follows from the above.
Results may differ from the reference program's by a relative error of at most 0.006.
Values may be sent and summed in bfloat16 or wider, within the bound.
A program may use at most 32 MiB of HBM per device.

```python
import math
import jax
import jax.numpy as jnp
from jax import lax

NDIR = 24
NFREQ = 25
LEV = 30
NBAND = 3
WXD = 128
WYD = 4
OX = 128
OY = 8
SLOT = 64
STEPS = 2
SPEC = 600
WY = 128
WX = 4096
OYG = 256
OXG = 4096
N_ROW = 32
N_COL = 32


def draw_mix_inverse(key, part):
    noise_key = jax.random.fold_in(key, 11)
    noise = jax.random.normal(noise_key, (LEV, LEV), jnp.float32)
    return 0.7 * jnp.eye(LEV, dtype=jnp.float32) + 0.3 * noise / jnp.sqrt(jnp.float32(LEV))


def draw_fold_index(key, part):
    total = OX * N_COL
    spread = jax.random.randint(jax.random.fold_in(key, 5), (N_COL, OX), 0, total, jnp.int32)
    within = jax.random.randint(jax.random.fold_in(key, 7), (N_COL,), 0, OX, jnp.int32)
    far_block = (jnp.arange(N_COL, dtype=jnp.int32) + N_COL // 2) % N_COL
    first = far_block * OX + within
    spread = spread.at[:, 0].set(first)
    return spread.reshape(-1).astype(jnp.int32)


def plant(result, own_key, smallest, high):
    longest = result.shape.index(max(result.shape))
    spots = []
    for shift in (0, 1):
        where = [jax.random.randint(jax.random.fold_in(own_key, axis), (), 0, length) for axis, length in enumerate(result.shape)]
        where[longest] = (where[longest] + shift) % result.shape[longest]
        spots.append(tuple(where))
    return result.at[spots[0]].set(smallest).at[spots[1]].set(high)


def block_scale(stream_key, dims, pieces, least, high):
    loudness, own = 1.0, jax.random.fold_in(stream_key, 6)
    for position, parts in pieces:
        steps = jnp.exp(jax.random.uniform(jax.random.fold_in(own, position), (parts,), jnp.float32, least / len(pieces), high / len(pieces)))
        loudness = loudness * jnp.repeat(steps, dims[position] // parts).reshape([-1 if axis == position else 1 for axis in range(len(dims))])
    return loudness


def bell_draw(own_key, dims, scale, reach, shards=(), kind=jnp.bfloat16):
    loudness = block_scale(own_key, dims, shards, -0.22, 0.18) if shards else 1.0
    drawn = jax.random.normal(own_key, dims, jnp.float32) * scale * loudness
    return jnp.minimum(jnp.maximum(drawn, -reach), reach).astype(kind)


def setup_inputs(seed: int = 0) -> dict:
    splits = jax.random.split(jax.random.key(seed), 23)
    spectra = jnp.clip(jnp.exp(math.log(1.0) - 4.61031033 * jax.random.uniform(splits[0], (SPEC, WY, WX), jnp.float32) ** block_scale(splits[0], (SPEC, WY, WX), ((1, 32), (2, 32)), -0.2, 0.2)), 0.0099487305, 1.0).astype(jnp.bfloat16)
    wind = bell_draw(splits[1], (2, WY, WX), 3.0, 18.0, ((1, 32), (2, 32)), jnp.float32)
    wave_current = bell_draw(splits[2], (3, WY, WX), 0.5, 3.0, ((1, 32), (2, 32)), jnp.float32)
    wave_wet = plant((jax.random.randint(splits[3], (WY, WX), 0, 4) < 3).astype(jnp.int32), jax.random.fold_in(splits[3], 1), 0, 1)
    interaction = bell_draw(splits[4], (SPEC, SPEC), SPEC ** -0.5, 0.25)
    input_rate = jnp.clip(jnp.exp(jax.random.uniform(splits[5], (NFREQ,), jnp.float32, math.log(0.002), math.log(0.03))), 0.002, 0.03)
    eta_gain = jnp.clip(jax.random.uniform(splits[6], (NFREQ,), jnp.float32, -0.5, 0.5), -0.5, 0.5)
    stress_map = bell_draw(splits[7], (2, SPEC), SPEC ** -0.5, 0.25, (), jnp.float32)
    stokes_map = bell_draw(splits[8], (2 * NBAND, SPEC), SPEC ** -0.5, 0.25, (), jnp.float32)
    ocean_vel = bell_draw(splits[9], (2, LEV, OYG, OXG), 0.5, 3.0, ((2, 32), (3, 32)), jnp.float32)
    ocean_eta = bell_draw(splits[10], (OYG, OXG), 0.5, 3.0, ((0, 32), (1, 32)), jnp.float32)
    ocean_wet = plant((jax.random.randint(splits[11], (OYG, OXG), 0, 3) < 2).astype(jnp.int32), jax.random.fold_in(splits[11], 1), 0, 1)
    coriolis = jnp.clip(jax.random.uniform(splits[12], (OYG, OXG), jnp.float32, -1.5, 1.5) * block_scale(splits[12], (OYG, OXG), ((0, 32), (1, 32)), -0.4, 0.0), -1.5, 1.5)
    tau_profile = jnp.clip(jnp.exp(jax.random.uniform(splits[13], (LEV,), jnp.float32, math.log(0.05), math.log(1.0))), 0.05, 1.0)
    stokes_profile = jnp.clip(jnp.exp(jax.random.uniform(splits[14], (NBAND, LEV), jnp.float32, math.log(0.05), math.log(1.0))), 0.05, 1.0)
    thickness = jnp.clip(jnp.exp(jax.random.uniform(splits[15], (LEV,), jnp.float32, math.log(0.02), math.log(0.1))), 0.02, 0.1)
    mix_inverse = draw_mix_inverse(jax.random.fold_in(splits[22], 71), 0)
    fold_index = draw_fold_index(jax.random.fold_in(splits[22], 71), 0)
    wave_send = plant(jax.random.randint(splits[18], (N_ROW, N_COL, 3, SLOT), 0, WYD * WXD), jax.random.fold_in(splits[18], 1), 0, (WYD * WXD) - 1).astype(jnp.int32)
    ocean_recv = bell_draw(splits[19], (N_ROW, N_COL, 3, SLOT, OY * OX), (3 * SLOT) ** -0.5, 0.4375, ((0, 32), (1, 32)))
    ocean_send = plant(jax.random.randint(splits[20], (N_ROW, N_COL, 3, SLOT), 0, OY * OX), jax.random.fold_in(splits[20], 1), 0, (OY * OX) - 1).astype(jnp.int32)
    wave_recv = bell_draw(splits[21], (N_ROW, N_COL, 3, SLOT, WYD * WXD), (3 * SLOT) ** -0.5, 0.4375, ((0, 32), (1, 32)))
    return dict(spectra=spectra, wind=wind, wave_current=wave_current, wave_wet=wave_wet, interaction=interaction, input_rate=input_rate, eta_gain=eta_gain, stress_map=stress_map, stokes_map=stokes_map, ocean_vel=ocean_vel, ocean_eta=ocean_eta, ocean_wet=ocean_wet, coriolis=coriolis, tau_profile=tau_profile, stokes_profile=stokes_profile, thickness=thickness, mix_inverse=mix_inverse, fold_index=fold_index, wave_send=wave_send, ocean_recv=ocean_recv, ocean_send=ocean_send, wave_recv=wave_recv)


viscous = 0.2
surface_rate = 0.5
highest = lax.Precision.HIGHEST


def wave_cells(energy, wind_cells, current, wet_cells, interaction, input_rate, eta_gain, stress_map, stokes_map):
    spectrum_len = energy.shape[0]
    heading = ((jnp.arange(spectrum_len) % NDIR).astype(jnp.float32) + 0.5) * (2.0 * math.pi / NDIR)
    cosine = jnp.cos(heading)[:, None]
    sine_dir = jnp.sin(heading)[:, None]
    relative = (wind_cells[0] - current[0]) * cosine + (wind_cells[1] - current[1]) * sine_dir
    growth = jnp.repeat(input_rate, NDIR)[:, None] * jax.nn.softplus(relative)
    energy_wide = energy.astype(jnp.float32)
    transfer_term = jnp.dot(interaction, energy, preferred_element_type=jnp.float32)
    level_term = jnp.repeat(eta_gain, NDIR)[:, None] * current[2]
    updated = (wet_cells.astype(jnp.float32) * (energy_wide + (growth + level_term) * energy_wide + transfer_term)).astype(jnp.bfloat16)
    stress = jnp.dot(stress_map, growth * energy_wide, precision=highest)
    stokes = jnp.dot(stokes_map, updated.astype(jnp.float32), precision=highest)
    return updated, jnp.concatenate([stress, stokes], 0).astype(jnp.bfloat16)


def ocean_force(velocity, forcing, ocean_wet, coriolis, tau_profile, stokes_profile):
    wet_mask = ocean_wet.astype(jnp.float32)
    along_u = tau_profile[:, None, None] * forcing[0]
    along_v = tau_profile[:, None, None] * forcing[1]
    for band_index in range(NBAND):
        profile = stokes_profile[band_index][:, None, None]
        along_u = along_u + coriolis * profile * forcing[3 + 2 * band_index]
        along_v = along_v - coriolis * profile * forcing[2 + 2 * band_index]
    return wet_mask * (velocity + jnp.stack([along_u, along_v]))


def ocean_finish(forced, padded, elevation, ocean_wet, thickness, mix_inverse):
    wet_mask = ocean_wet.astype(jnp.float32)
    laplacian = padded[:, :, 2:, 1:-1] + padded[:, :, :-2, 1:-1] + padded[:, :, 1:-1, 2:] + padded[:, :, 1:-1, :-2] - 4.0 * forced
    smoothed = wet_mask * (forced + viscous * laplacian)
    transport = jnp.einsum('l,clyx->cyx', thickness, padded, precision=highest)
    divergence = 0.5 * (transport[0, 1:-1, 2:] - transport[0, 1:-1, :-2]) + 0.5 * (transport[1, 2:, 1:-1] - transport[1, :-2, 1:-1])
    eta_next = wet_mask * (elevation - surface_rate * divergence)
    vel_next = jnp.einsum('lm,cmyx->clyx', mix_inverse, smoothed, precision=highest)
    return vel_next, eta_next


def tile_view(grid_data, tile_rows, tile_cols):
    fields = grid_data.shape[0]
    shaped = grid_data.reshape(fields, N_ROW, tile_rows, N_COL, tile_cols)
    return shaped.transpose(1, 3, 0, 2, 4).reshape(N_ROW, N_COL, fields, tile_rows * tile_cols)


def grid_view(tile_data, tile_rows, tile_cols):
    fields = tile_data.shape[2]
    shaped = tile_data.reshape(N_ROW, N_COL, fields, tile_rows, tile_cols)
    return shaped.transpose(2, 0, 3, 1, 4).reshape(fields, N_ROW * tile_rows, N_COL * tile_cols)


def pick_slots(tile_data, indices):
    return jnp.moveaxis(jnp.take(tile_data, indices, axis=1), 1, 0)


def remap_tiles(tiles, send_rows, weights):
    slot_rows = jax.vmap(jax.vmap(pick_slots))(tiles, send_rows)
    zero_band = jnp.zeros_like(slot_rows[:1, :, 0])
    from_north = jnp.concatenate([slot_rows[1:, :, 0], zero_band], 0)
    from_south = jnp.concatenate([zero_band, slot_rows[:-1, :, 2]], 0)
    received = jnp.stack([from_north, slot_rows[:, :, 1], from_south], axis=2)

    def band_sum(items):
        return jnp.einsum('cjfs,cjsn->cfn', items[0].astype(jnp.float32), items[1].astype(jnp.float32))

    return lax.map(band_sum, (received, weights))


def pad_grid(forced, fold_index):
    north_row = -jnp.take(forced[:, :, -1, :], fold_index, axis=2)[:, :, None, :]
    south_row = jnp.zeros_like(north_row)
    middle = jnp.concatenate([south_row, forced, north_row], axis=2)
    return jnp.concatenate([middle[..., -1:], middle, middle[..., :1]], axis=3)


def reference(spectra, wind, wave_current, wave_wet, interaction, input_rate, eta_gain, stress_map, stokes_map, ocean_vel, ocean_eta, ocean_wet, coriolis, tau_profile, stokes_profile, thickness, mix_inverse, fold_index, wave_send, ocean_recv, ocean_send, wave_recv):
    energy = tile_view(spectra, WYD, WXD)
    wind_tiles = tile_view(wind, WYD, WXD)
    current = tile_view(wave_current, WYD, WXD)
    wet_tiles = tile_view(wave_wet[None], WYD, WXD)[:, :, 0]
    velocity = ocean_vel
    elevation = ocean_eta
    tile_step = jax.vmap(wave_cells, in_axes=(0, 0, 0, 0, None, None, None, None, None))

    def band_step(items):
        return tile_step(items[0], items[1], items[2], items[3], interaction, input_rate, eta_gain, stress_map, stokes_map)

    for step_index in range(STEPS):
        energy, fields = lax.map(band_step, (energy, wind_tiles, current, wet_tiles))
        forcing = grid_view(remap_tiles(fields, wave_send, ocean_recv), OY, OX)
        forced = ocean_force(velocity, forcing, ocean_wet, coriolis, tau_profile, stokes_profile)
        velocity, elevation = ocean_finish(forced, pad_grid(forced, fold_index), elevation, ocean_wet, thickness, mix_inverse)
        back = jnp.stack([velocity[0, 0], velocity[1, 0], elevation]).astype(jnp.bfloat16)
        current = remap_tiles(tile_view(back, OY, OX), ocean_send, wave_recv)
    return grid_view(energy, WYD, WXD), velocity, elevation, grid_view(current, WYD, WXD)
```

```python
import math

import jax
import jax.numpy as jnp
from jax import lax
from jax.experimental import pallas as pl
from jax.experimental.pallas import tpu as pltpu
from jax.sharding import PartitionSpec as P

NDIR = 24
NFREQ = 25
LEV = 30
NBAND = 3
STEPS = 2
SLOT = 64
SPEC = NDIR * NFREQ

viscous = 0.2
surface_rate = 0.5
highest = lax.Precision.HIGHEST
MESH = pl.DeviceIdType.MESH
f32 = jnp.float32
bf16 = jnp.bfloat16

KINDS = (
    ("slot", "n"), ("slot", "s"),
    ("key", "n"), ("key", "s"), ("key", "e"), ("key", "w"),
    ("bulk", "n"), ("bulk", "s"), ("bulk", "e"), ("bulk", "w"),
    ("back", "n"), ("back", "s"),
)


def iota(shape, dim):
    return lax.broadcasted_iota(jnp.int32, shape, dim)


def split2(x):
    high = x.astype(bf16)
    low = (x - high.astype(f32)).astype(bf16)
    return high, low


def kernel(
    *refs,
):
    inputs, refs = refs[:22], refs[22:]
    spec_out, vel_out, eta_out, cur_out = refs[:4]
    local, refs = refs[4:26], refs[26:]
    (
        spec_v, wind_ref, cur_ref, wwet_ref, inter_v, rate_ref, gain_ref, stress_ref, stokes_ref,
        vel_v, eta_ref, owet_ref, cor_ref, tau_ref, sprof_ref, thick_ref, mix_ref, fold_ref,
        wsend_ref, orecv_v, osend_ref, wrecv_v,
    ) = local
    (
    wide, energy, transfer, maps16, mall, proj, speed, cos_s, windbuf, curbuf, wwet8,
    whot, ohot, idxbuf, fhot,
    rows_s, tpose, mixp, kmat, coef, orow, fw, vw, kv, forc, keys, backv, forced, smooth,
    sel, ins,
    slot_send, slot_recv, key_send, key_recv, bulk_send, bulk_recv, back_send, back_recv,
    kf_send, kf_all, vwf_send, vwf_all, fold_f,
    ssem, rsem, fs_sem, fr_sem, lsem,
    ) = refs
    n_row, n_col = lax.axis_size("row"), lax.axis_size("col")
    row, col = lax.axis_index("row"), lax.axis_index("col")
    north = (lax.rem(row + 1, n_row), col)
    south = (lax.rem(row + n_row - 1, n_row), col)
    east = (row, lax.rem(col + 1, n_col))
    west = (row, lax.rem(col + n_col - 1, n_col))
    at = {"n": north, "s": south, "e": east, "w": west}
    top = row == n_row - 1
    bottom = row == 0
    barrier = pltpu.get_barrier_semaphore()

    def peer(i):
        return lax.rem(col + i, n_col)

    def signal_to(device):
        pl.semaphore_signal(barrier, inc=1, device_id=device, device_id_type=MESH)

    signal_to(north)
    signal_to(south)

    @pl.when(jnp.logical_not(top))
    def _():
        signal_to(east)
        signal_to(west)

    @pl.when(top)
    def _():
        def tell(i, carry):
            signal_to((row, peer(i)))
            return carry

        lax.fori_loop(1, n_col, tell, 0)

    loads = [pltpu.make_async_copy(src, dst, lsem.at[i]) for i, (src, dst) in enumerate(zip(inputs, local))]
    early = (1, 2, 3, 5, 6, 7, 8, 18)
    for i in early + (0, 4, 10, 11, 12, 13, 14, 15, 16, 17, 20, 9, 19, 21):
        loads[i].start()

    def message(step, kind, way):
        place = step * len(KINDS) + KINDS.index((kind, way))
        index = {"n": 0, "s": 1, "e": 2, "w": 3}[way]
        if kind == "slot":
            src, dst = slot_send.at[step, index], slot_recv.at[step, index]
        elif kind == "key":
            src, dst = key_send.at[step, min(index, 2)], key_recv.at[step, index]
        elif kind == "bulk":
            src, dst = bulk_send.at[step, min(index, 2)], bulk_recv.at[step, index]
        else:
            src, dst = back_send.at[step, index], back_recv.at[step, index]
        return pltpu.make_async_remote_copy(
            src_ref=src, dst_ref=dst, send_sem=ssem.at[place], recv_sem=rsem.at[place],
            device_id=at[way], device_id_type=MESH,
        )

    def fold_copy(step, kind, i):
        src, whole = (kf_send, kf_all) if kind == 0 else (vwf_send, vwf_all)
        place = pl.ds(pl.multiple_of(col * 128, 128), 128)
        return pltpu.make_async_remote_copy(
            src_ref=src.at[step], dst_ref=whole.at[step, :, place],
            send_sem=fs_sem.at[step, kind, i], recv_sem=fr_sem.at[step, kind, col],
            device_id=(row, peer(i)), device_id_type=MESH,
        )

    def fold_wait_recv(step, kind):
        src, whole = (kf_send, kf_all) if kind == 0 else (vwf_send, vwf_all)

        def wait_one(i, carry):
            other = peer(i)
            place = pl.ds(pl.multiple_of(other * 128, 128), 128)
            pltpu.make_async_remote_copy(
                src_ref=src.at[step], dst_ref=whole.at[step, :, place],
                send_sem=fs_sem.at[step, kind, i], recv_sem=fr_sem.at[step, kind, other],
                device_id=(row, other), device_id_type=MESH,
            ).wait_recv()
            return carry

        lax.fori_loop(1, n_col, wait_one, 0)

    def fold_start(step, kind):
        def start_one(i, carry):
            fold_copy(step, kind, i).start()
            return carry

        lax.fori_loop(1, n_col, start_one, 0)

    def fold_wait_send(step, kind):
        def wait_one(i, carry):
            fold_copy(step, kind, i).wait_send()
            return carry

        lax.fori_loop(1, n_col, wait_one, 0)

    for i in early:
        loads[i].wait()
    heading = (iota((NDIR, 128), 0).astype(f32) + 0.5) * (2.0 * math.pi / NDIR)
    cos_s[0] = jnp.cos(heading)
    cos_s[1] = jnp.sin(heading)
    windbuf[...] = jnp.zeros_like(windbuf)
    curbuf[...] = jnp.zeros_like(curbuf)
    for y in range(4):
        lanes = slice(y * 128, (y + 1) * 128)
        for i in range(2):
            windbuf[i : i + 1, lanes] = wind_ref[i, y : y + 1, :]
        for i in range(3):
            curbuf[i : i + 1, lanes] = cur_ref[i, y : y + 1, :]
        wet = jnp.broadcast_to(wwet_ref[y : y + 1, :].astype(f32), (8, 128))
        wwet8[:, lanes] = jnp.where(iota((8, 128), 0) < 2, 1.0, wet)

    def speeds():
        rel_x = windbuf[0:1, :] - curbuf[0:1, :]
        rel_y = windbuf[1:2, :] - curbuf[1:2, :]
        for y in range(4):
            lanes = slice(y * 128, (y + 1) * 128)
            relative = rel_x[:, lanes] * cos_s[0] + rel_y[:, lanes] * cos_s[1]
            speed[:, lanes] = jnp.maximum(relative, 0.0) + jnp.log(1.0 + jnp.exp(-jnp.abs(relative)))

    speeds()

    def one_hot(send_ref, cells):
        idxbuf[...] = jnp.full(idxbuf.shape, -1, jnp.int32)
        for j in range(3):
            idxbuf[0:1, j * 128 : j * 128 + SLOT] = send_ref[j]
        hot = iota((cells, 3 * 128), 0) == idxbuf[0:1, :]
        return jnp.where(hot, 1.0, 0.0).astype(bf16)

    whot[...] = one_hot(wsend_ref, 512)

    maps16[0:2, :] = stress_ref[...]
    maps16[2:8, :] = stokes_ref[...]
    maps16[8:10, :] = stress_ref[...]
    maps16[10:16, :] = stokes_ref[...]
    place = iota((16, SPEC), 1)
    freq = ((place.astype(f32) + 0.5) * (1.0 / NDIR)).astype(jnp.int32)
    direction = place - freq * NDIR
    rate_wide = jnp.zeros((16, SPEC), f32)
    gain_wide = jnp.zeros((16, SPEC), f32)
    for f in range(NFREQ):
        rate_wide = jnp.where(freq == f, rate_ref[0, f], rate_wide)
        gain_wide = jnp.where(freq == f, gain_ref[0, f], gain_wide)
    row16 = iota((16, SPEC), 0)
    half = jnp.where(row16 >= 8, 1, 0)
    maps = maps16[...]
    rated = maps * rate_wide
    for pair in range(12):
        high, low = split2(jnp.where(direction == 2 * pair + half, rated, 0.0))
        mall[pair * 16 : pair * 16 + 16, :] = high
        mall[208 + pair * 16 : 208 + pair * 16 + 16, :] = low

    loads[0].wait()
    wide[...] = spec_v[...].astype(f32)
    for y in range(4):
        energy[0, :, y * 128 : (y + 1) * 128] = wide[pl.ds(y, SPEC, stride=4), :].astype(bf16)

    loads[4].wait()
    inter = inter_v[...]
    first = maps.astype(bf16)
    rest = maps - first.astype(f32)
    second = rest.astype(bf16)
    third = (rest - second.astype(f32)).astype(bf16)
    moved = (
        jnp.dot(first, inter, preferred_element_type=f32)
        + jnp.dot(second, inter, preferred_element_type=f32)
        + jnp.dot(third, inter, preferred_element_type=f32)
    )
    last_pair = jnp.where(row16 < 8, maps + moved, maps * gain_wide)
    last_pair = jnp.where((row16 < 2) | ((row16 >= 8) & (row16 < 10)), 0.0, last_pair)
    high, low = split2(last_pair)
    mall[192:208, :] = high
    mall[400:416, :] = low

    def project(step):
        both = jnp.dot(mall[...], energy[step], preferred_element_type=f32)
        proj[...] = both[0:208] + both[208:416]

    def send_slots(step):
        total = proj[192:200, :] + curbuf[2:3, :] * proj[200:208, :]
        for k in range(NDIR):
            total = total + speed[k : k + 1, :] * proj[8 * k : 8 * k + 8, :]
        fields = (total * wwet8[...]).astype(bf16)
        slots = jnp.dot(fields, whot[...], preferred_element_type=f32)
        slot_send[step, 1] = slots[:, 0:128]
        slot_send[step, 0] = slots[:, 256:384]
        return slots[:, 128 : 128 + SLOT].astype(bf16)

    project(0)
    own_slots = send_slots(0)

    @pl.when(jnp.logical_not(top))
    def _():
        pl.semaphore_wait(barrier, 4)

    @pl.when(top)
    def _():
        pl.semaphore_wait(barrier, n_col + 1)

    def start(step, kind):
        sent = [message(step, kind, way) for k, way in KINDS if k == kind]
        for copy in sent:
            copy.start()
        return sent

    pending = []
    slot_msgs = start(0, "slot")
    pending += slot_msgs

    for i in (10, 11, 12, 13, 14, 15, 16, 17, 20):
        loads[i].wait()
    for y in range(8):
        lanes = slice(y * 128, (y + 1) * 128)
        wet = owet_ref[y : y + 1, :].astype(f32)
        orow[0:1, lanes] = wet
        wet8 = jnp.broadcast_to(wet, (8, 128))
        cor8 = jnp.broadcast_to(cor_ref[y : y + 1, :], (8, 128))
        fw[:, lanes] = jnp.where(iota((8, 128), 0) < 2, wet8, wet8 * cor8)
        backv[:, lanes] = jnp.broadcast_to(eta_ref[y : y + 1, :], (8, 128))
    rows_s[...] = jnp.zeros_like(rows_s)
    rows_s[0:1, 0:LEV] = mix_ref[0:1, :]
    rows_s[1:2, 0:LEV] = tau_ref[...]
    rows_s[2:5, 0:LEV] = sprof_ref[...]
    rows_s[5:6, 0:LEV] = thick_ref[...]
    mixp[...] = jnp.zeros_like(mixp)
    mixp[0:LEV, 0:LEV] = mix_ref[...]

    def wide_row(i):
        return jnp.broadcast_to(rows_s[i : i + 1, :], (8, 128))

    r8 = iota((8, 128), 0)
    lane8 = iota((8, 128), 1)
    along_u = jnp.where(r8 == 0, wide_row(1), 0.0)
    along_v = jnp.where(r8 == 1, wide_row(1), 0.0)
    for b in range(NBAND):
        along_u = jnp.where(r8 == 3 + 2 * b, wide_row(2 + b), along_u)
        along_v = jnp.where(r8 == 2 + 2 * b, -wide_row(2 + b), along_v)
    tpose[...] = jnp.zeros_like(tpose)
    tpose[0:8, :] = along_u
    tpose[8:16, :] = along_v
    turned = jnp.transpose(tpose[...])
    gain_u = turned[0:32, 0:8]
    gain_v = turned[0:32, 8:16]
    m0, thick = wide_row(0), wide_row(5)
    for i, (profile, weight) in enumerate(((along_u, m0), (along_v, m0), (along_u, thick), (along_v, thick))):
        coef[i] = jnp.broadcast_to(jnp.sum(profile * weight, axis=1, keepdims=True), (8, 128))
    m0_far = pltpu.roll(m0, 32, 1)
    thick_far = pltpu.roll(thick, 32, 1)
    kmat[...] = jnp.where(
        r8 == 0, m0, jnp.where(r8 == 1, m0_far, jnp.where(r8 == 2, thick, jnp.where(r8 == 3, thick_far, 0.0)))
    )

    cell = iota((1024, 128), 0)
    spot = iota((1024, 128), 1)
    edge = jnp.where(spot < 8, spot * 128 + 127, jnp.where(spot < 16, (spot - 8) * 128, -1))
    sel[...] = jnp.where(cell == edge, 1.0, 0.0).astype(bf16)
    cell_t = iota((128, 1024), 1)
    spot_t = iota((128, 1024), 0)
    edge_t = jnp.where(spot_t < 8, spot_t * 128, jnp.where(spot_t < 16, (spot_t - 8) * 128 + 127, -1))
    ins[...] = jnp.where(cell_t == edge_t, 1.0, 0.0).astype(bf16)

    ohot[...] = one_hot(osend_ref, 1024)

    @pl.when(top)
    def _():
        hot = iota((n_col * 128, 128), 0) == fold_ref[...]
        fhot[...] = jnp.where(hot, 1.0, 0.0).astype(bf16)

    def prepare_ocean(step):
        kv[...] = jnp.dot(kmat[:, 0:64], vw[...], precision=highest, preferred_element_type=f32)

        @pl.when(top)
        def _():
            line = vw[:, 7 * 128 : 8 * 128].astype(bf16)
            vwf_send[step] = line
            vwf_all[step, :, pl.ds(pl.multiple_of(col * 128, 128), 128)] = line
            fold_start(step, 1)

    loads[9].wait()
    vw[...] = jnp.zeros_like(vw)
    for c in range(2):
        for y in range(8):
            lanes = slice(y * 128, (y + 1) * 128)
            level = vel_v[pl.ds(c * 8 * LEV + y, LEV, stride=8), :]
            vw[c * 32 : c * 32 + LEV, lanes] = level * orow[0:1, lanes]
    prepare_ocean(0)

    def next_transfer(step):
        transfer[...] = jnp.dot(inter_v[...], energy[step], preferred_element_type=f32)

    def update_energy(step):
        level = curbuf[2:3, :]
        wet = wwet8[2:3, :]
        for pair in range(13):
            count = 2 if pair < 12 else 1
            rows = slice(pair * 48, pair * 48 + 24 * count)
            old = energy[step, rows, :].astype(f32)
            parts = []
            for part in range(count):
                f = 2 * pair + part
                e = old[part * 24 : part * 24 + 24]
                t = transfer[f * 24 : f * 24 + 24, :]
                factor = rate_ref[0, f] * speed[...] + gain_ref[0, f] * level
                parts.append(wet * (e + factor * e + t))
            new = parts[0] if count == 1 else jnp.concatenate(parts, axis=0)
            if step == STEPS - 1:
                base, size = pair * 192, 96 * count
                for y in range(4):
                    wide[pl.ds(base + y, 24 * count, stride=4), :] = new[:, y * 128 : (y + 1) * 128]
                spec_out[base : base + size, :] = wide[base : base + size, :].astype(bf16)
            else:
                energy[step + 1, rows, :] = new.astype(bf16)

    next_transfer(0)
    update_energy(0)
    loads[19].wait()
    loads[21].wait()

    def pass_north(step, own_slots, slot_msgs):
        for copy in slot_msgs:
            copy.wait_recv()
        from_south = jnp.where(bottom, 0.0, slot_recv[step, 0][:, 0:SLOT]).astype(bf16)
        from_north = jnp.where(top, 0.0, slot_recv[step, 1][:, 0:SLOT]).astype(bf16)
        force = (
            jnp.dot(from_north, orecv_v[0:64, :], preferred_element_type=f32)
            + jnp.dot(own_slots, orecv_v[64:128, :], preferred_element_type=f32)
            + jnp.dot(from_south, orecv_v[128:192, :], preferred_element_type=f32)
        )
        force = force * fw[...]
        forc[...] = force
        for y in range(8):
            lanes = slice(y * 128, (y + 1) * 128)
            tile = force[:, lanes]
            value = kv[:, lanes]
            for i in range(4):
                extra = jnp.sum(tile * coef[i], axis=0, keepdims=True)
                value = value + jnp.where(r8 == i, extra, 0.0)
            keys[y] = value
        key_send[step, 0] = keys[7]
        key_send[step, 1] = keys[0]
        edges = jnp.zeros((8, 128), f32)
        for y in range(8):
            edges = jnp.where(lane8 == y, pltpu.roll(keys[y], y + 1, 1), edges)
            edges = jnp.where(lane8 == 8 + y, pltpu.roll(keys[y], 8 + y, 1), edges)
        key_send[step, 2] = edges
        msgs = start(step, "key")

        @pl.when(top)
        def _():
            line = jnp.concatenate([keys[7], forc[:, 7 * 128 : 8 * 128]], axis=0).astype(bf16)
            kf_send[step] = line
            kf_all[step, :, pl.ds(pl.multiple_of(col * 128, 128), 128)] = line
            fold_start(step, 0)

        force = forc[...]
        for c, gain in enumerate((gain_u, gain_v)):
            forced[c * 32 : c * 32 + 32, :] = vw[c * 32 : c * 32 + 32, :] + jnp.dot(
                gain, force, precision=highest, preferred_element_type=f32
            )
        low = forced[...].astype(bf16)
        bulk_send[step, 0] = low[:, 7 * 128 : 8 * 128]
        bulk_send[step, 1] = low[:, 0:128]
        bulk_send[step, 2] = jnp.dot(low, sel[...], preferred_element_type=f32).astype(bf16)
        bulks = start(step, "bulk")
        return msgs, bulks

    def finish_keys(step, msgs):
        for copy in msgs:
            copy.wait_recv()

        @pl.when(top)
        def _():
            fold_wait_recv(step, 0)
            chosen = jnp.dot(kf_all[step], fhot[...], preferred_element_type=f32)
            key_recv[step, 1] = -chosen[0:8]
            fold_f[...] = chosen[8:16]

        south_halo = jnp.where(bottom, 0.0, key_recv[step, 0])
        north_halo = key_recv[step, 1]
        from_west = key_recv[step, 2]
        from_east = key_recv[step, 3]
        backs = []
        for y in range(8):
            lanes = slice(y * 128, (y + 1) * 128)
            here = keys[y]
            up = keys[y + 1] if y < 7 else north_halo
            down = keys[y - 1] if y > 0 else south_halo
            left_in = from_west if y == 0 else pltpu.roll(from_west, 128 - y, 1)
            right_in = pltpu.roll(from_east, 127 - (8 + y), 1)
            left = jnp.where(lane8 == 0, left_in, pltpu.roll(here, 1, 1))
            right = jnp.where(lane8 == 127, right_in, pltpu.roll(here, 127, 1))
            wet = jnp.broadcast_to(orow[0:1, lanes], (8, 128))
            level = here + viscous * (up + down + left + right - 4.0 * here)
            spread = 0.5 * (right - left) + 0.5 * pltpu.roll(up - down, 7, 0)
            elevation = backv[:, lanes] - surface_rate * spread
            value = wet * jnp.where(r8 < 2, level, jnp.where(r8 == 2, elevation, 0.0))
            backv[:, lanes] = value
            if step == STEPS - 1:
                eta_out[y : y + 1, :] = value[2:3, :]
        slots = jnp.dot(backv[...].astype(bf16), ohot[...], preferred_element_type=f32)
        back_send[step, 1] = slots[:, 0:128]
        back_send[step, 0] = slots[:, 256:384]
        own = slots[:, 128 : 128 + SLOT].astype(bf16)
        return own, start(step, "back")

    def finish_current(step, own, msgs):
        for copy in msgs:
            copy.wait_recv()
        from_south = jnp.where(bottom, 0.0, back_recv[step, 0][:, 0:SLOT]).astype(bf16)
        from_north = jnp.where(top, 0.0, back_recv[step, 1][:, 0:SLOT]).astype(bf16)
        curbuf[...] = (
            jnp.dot(from_north, wrecv_v[0:64, :], preferred_element_type=f32)
            + jnp.dot(own, wrecv_v[64:128, :], preferred_element_type=f32)
            + jnp.dot(from_south, wrecv_v[128:192, :], preferred_element_type=f32)
        )

    def finish_velocity(step, bulks):
        for copy in bulks:
            copy.wait_recv()

        @pl.when(top)
        def _():
            fold_wait_recv(step, 1)
            chosen = jnp.dot(vwf_all[step], fhot[...], preferred_element_type=f32)
            added = jnp.concatenate(
                [
                    jnp.dot(gain, fold_f[...], precision=highest, preferred_element_type=f32)
                    for gain in (gain_u, gain_v)
                ],
                axis=0,
            )
            bulk_recv[step, 1] = (-(chosen + added)).astype(bf16)

        south_halo = jnp.where(bottom, 0.0, bulk_recv[step, 0].astype(f32))
        north_halo = bulk_recv[step, 1].astype(f32)
        lane64 = iota((64, 128), 1)
        sides = jnp.where(lane64 < 8, bulk_recv[step, 2].astype(f32), bulk_recv[step, 3].astype(f32))
        outer = jnp.dot(sides.astype(bf16), ins[...], preferred_element_type=f32)
        for y in range(8):
            lanes = slice(y * 128, (y + 1) * 128)
            here = forced[:, lanes]
            up = forced[:, (y + 1) * 128 : (y + 2) * 128] if y < 7 else north_halo
            down = forced[:, (y - 1) * 128 : y * 128] if y > 0 else south_halo
            left = jnp.where(lane64 == 0, 0.0, pltpu.roll(here, 1, 1))
            right = jnp.where(lane64 == 127, 0.0, pltpu.roll(here, 127, 1))
            around = up + down + left + right + outer[:, lanes] - 4.0 * here
            smooth[:, lanes] = orow[0:1, lanes] * (here + viscous * around)
        for c in range(2):
            new = jnp.dot(
                mixp[...], smooth[c * 32 : c * 32 + 32, :], precision=highest, preferred_element_type=f32
            )
            if step == STEPS - 1:
                for y in range(8):
                    vel_out[pl.ds(c * 8 * LEV + y, LEV, stride=8), :] = new[0:LEV, y * 128 : (y + 1) * 128]
            else:
                vw[c * 32 : c * 32 + 32, :] = new * orow[0:1, :]

    for step in range(STEPS):
        keys_sent, bulks = pass_north(step, own_slots, slot_msgs)
        pending += keys_sent + bulks
        if step == 0:
            project(1)
        else:
            update_energy(step)
        own_back, backs = finish_keys(step, keys_sent)
        pending += backs
        if step == 0:
            next_transfer(1)
        else:
            finish_velocity(step, bulks)
        finish_current(step, own_back, backs)
        if step == 0:
            speeds()
            own_slots = send_slots(1)
            slot_msgs = start(1, "slot")
            pending += slot_msgs
            finish_velocity(step, bulks)
            prepare_ocean(1)
    for y in range(4):
        for i in range(3):
            cur_out[i, y : y + 1, :] = curbuf[i : i + 1, y * 128 : (y + 1) * 128]
    for copy in pending:
        copy.wait_send()

    @pl.when(top)
    def _():
        for step in range(STEPS):
            for kind in range(2):
                fold_wait_send(step, kind)


def shards(
    spectra, wind, wave_current, wave_wet, interaction, input_rate, eta_gain, stress_map, stokes_map,
    ocean_vel, ocean_eta, ocean_wet, coriolis, tau_profile, stokes_profile, thickness, mix_inverse,
    fold_index, wave_send, ocean_recv, ocean_send, wave_recv,
):
    n_col = lax.axis_size("col")
    vmem = pl.BlockSpec(memory_space=pltpu.VMEM)
    hbm = pl.BlockSpec(memory_space=pltpu.HBM)
    V = pltpu.VMEM
    scratch = [
        V((2400, 128), f32), V((STEPS, SPEC, 512), bf16), V((SPEC, 512), f32), V((16, SPEC), f32),
        V((416, SPEC), bf16), V((208, 512), f32), V((NDIR, 512), f32), V((2, NDIR, 128), f32),
        V((8, 512), f32), V((8, 512), f32), V((8, 512), f32),
        V((512, 384), bf16), V((1024, 384), bf16), V((1, 384), jnp.int32), V((n_col * 128, 128), bf16),
        V((8, 128), f32), V((128, 128), f32), V((32, 32), f32), V((8, 128), f32), V((4, 8, 128), f32),
        V((1, 1024), f32), V((8, 1024), f32), V((64, 1024), f32), V((8, 1024), f32), V((8, 1024), f32),
        V((8, 8, 128), f32), V((8, 1024), f32), V((64, 1024), f32), V((64, 1024), f32),
        V((1024, 128), bf16), V((128, 1024), bf16),
        V((STEPS, 2, 8, 128), f32), V((STEPS, 2, 8, 128), f32),
        V((STEPS, 3, 8, 128), f32), V((STEPS, 4, 8, 128), f32),
        V((STEPS, 3, 64, 128), bf16), V((STEPS, 4, 64, 128), bf16),
        V((STEPS, 2, 8, 128), f32), V((STEPS, 2, 8, 128), f32),
        V((STEPS, 16, 128), bf16), V((STEPS, 16, n_col * 128), bf16),
        V((STEPS, 64, 128), bf16), V((STEPS, 64, n_col * 128), bf16), V((8, 128), f32),
        pltpu.SemaphoreType.DMA((STEPS * len(KINDS),)), pltpu.SemaphoreType.DMA((STEPS * len(KINDS),)),
        pltpu.SemaphoreType.DMA((STEPS, 2, n_col)), pltpu.SemaphoreType.DMA((STEPS, 2, n_col)),
        pltpu.SemaphoreType.DMA((22,)),
    ]
    operands = (
        spectra.reshape(2400, 128), wind, wave_current, wave_wet, interaction,
        input_rate.reshape(1, NFREQ), eta_gain.reshape(1, NFREQ), stress_map, stokes_map,
        ocean_vel.reshape(480, 128), ocean_eta, ocean_wet, coriolis,
        tau_profile.reshape(1, LEV), stokes_profile, thickness.reshape(1, LEV), mix_inverse,
        fold_index.reshape(1, 128),
        wave_send.reshape(3, 1, SLOT), ocean_recv.reshape(192, 1024),
        ocean_send.reshape(3, 1, SLOT), wave_recv.reshape(192, 512),
    )
    held = [(pltpu.SMEM if i in (5, 6) else V)(x.shape, x.dtype) for i, x in enumerate(operands)]
    spec_out, vel_out, eta_out, cur_out = pl.pallas_call(
        kernel,
        name="coupled",
        out_shape=(
            jax.ShapeDtypeStruct((2400, 128), bf16),
            jax.ShapeDtypeStruct((480, 128), f32),
            jax.ShapeDtypeStruct((8, 128), f32),
            jax.ShapeDtypeStruct((3, 4, 128), f32),
        ),
        in_specs=[hbm] * len(operands),
        out_specs=(vmem, vmem, vmem, vmem),
        scratch_shapes=held + scratch,
        compiler_params=pltpu.CompilerParams(
            collective_id=0, has_side_effects=True, vmem_limit_bytes=40 * 1024 * 1024
        ),
    )(*[pltpu.with_memory_space_constraint(x, pltpu.HBM) for x in operands])
    return (
        spec_out.reshape(SPEC, 4, 128),
        vel_out.reshape(2, LEV, 8, 128),
        eta_out,
        cur_out,
    )


def solution(mesh):
    tiled3 = P(None, "row", "col")
    tiled = P("row", "col")
    in_specs = (
        tiled3, tiled3, tiled3, tiled, P(), P(), P(), P(), P(),
        P(None, None, "row", "col"), tiled, tiled, tiled, P(), P(), P(), P(), P("col"),
        P("row", "col", None, None), P("row", "col", None, None, None),
        P("row", "col", None, None), P("row", "col", None, None, None),
    )
    out_specs = (tiled3, P(None, None, "row", "col"), tiled, tiled3)
    return jax.shard_map(shards, mesh=mesh, in_specs=in_specs, out_specs=out_specs, check_vma=False)
```

```python
import math

import jax
import jax.numpy as jnp
from jax import lax
from jax.experimental import pallas as pl
from jax.experimental.pallas import tpu as pltpu
from jax.sharding import PartitionSpec as P

NDIR = 24
NFREQ = 25
LEV = 30
NBAND = 3
STEPS = 2
SLOT = 64
SPEC = NDIR * NFREQ
GROUP = 4

viscous = 0.2
surface_rate = 0.5
highest = lax.Precision.HIGHEST
MESH = pl.DeviceIdType.MESH
f32 = jnp.float32
bf16 = jnp.bfloat16

KINDS = (
    ("slot", "n"), ("slot", "s"),
    ("key", "n"), ("key", "s"), ("key", "e"), ("key", "w"),
    ("bulk", "n"), ("bulk", "s"), ("bulk", "e"), ("bulk", "w"),
    ("back", "n"), ("back", "s"),
)


def iota(shape, dim):
    return lax.broadcasted_iota(jnp.int32, shape, dim)


def split2(x):
    high = x.astype(bf16)
    low = (x - high.astype(f32)).astype(bf16)
    return high, low


def kernel(
    *refs,
):
    inputs, refs = refs[:22], refs[22:]
    spec_out, vel_out, eta_out, cur_out = refs[:4]
    local, refs = refs[4:26], refs[26:]
    (
        spec_v, wind_ref, cur_ref, wwet_ref, inter_v, rate_ref, gain_ref, stress_ref, stokes_ref,
        vel_v, eta_ref, owet_ref, cor_ref, tau_ref, sprof_ref, thick_ref, mix_ref, fold_ref,
        wsend_ref, orecv_v, osend_ref, wrecv_v,
    ) = local
    (
    wide, energy, transfer, maps16, mall, proj, speed, cos_s, windbuf, curbuf, wwet8,
    whot, ohot, idxbuf, fhot,
    rows_s, tpose, mixp, kmat, coef, orow, fw, vw, kv, forc, keys, backv, forced, smooth,
    sel, ins,
    slot_send, slot_recv, key_send, key_recv, bulk_send, bulk_recv, back_send, back_recv,
    kf_send, kf_all, line_send, lines, chosen_send, chosen_all, index_send, index_all, lhot,
    ssem, rsem, fs_sem, fr_sem, far_s, far_r, near_s, near_r, index_s, index_r, lsem,
    ) = refs
    n_row, n_col = lax.axis_size("row"), lax.axis_size("col")
    row, col = lax.axis_index("row"), lax.axis_index("col")
    north = (lax.rem(row + 1, n_row), col)
    south = (lax.rem(row + n_row - 1, n_row), col)
    east = (row, lax.rem(col + 1, n_col))
    west = (row, lax.rem(col + n_col - 1, n_col))
    at = {"n": north, "s": south, "e": east, "w": west}
    top = row == n_row - 1
    bottom = row == 0
    barrier = pltpu.get_barrier_semaphore()

    def peer(i):
        return lax.rem(col + i, n_col)

    def signal_to(device):
        pl.semaphore_signal(barrier, inc=1, device_id=device, device_id_type=MESH)

    @pl.when(jnp.logical_not(bottom))
    def _():
        signal_to(south)

    @pl.when(jnp.logical_not(top))
    def _():
        signal_to(north)
        signal_to(east)
        signal_to(west)

    @pl.when(top)
    def _():
        def tell(i, carry):
            signal_to((row, peer(i)))
            return carry

        lax.fori_loop(1, n_col, tell, 0)

    loads = [pltpu.make_async_copy(src, dst, lsem.at[i]) for i, (src, dst) in enumerate(zip(inputs, local))]
    early = (1, 2, 3, 5, 6, 7, 8, 18)
    for i in early + (0, 4, 10, 11, 12, 13, 14, 15, 16, 17, 20, 9, 19, 21):
        loads[i].start()

    def message(step, kind, way):
        place = step * len(KINDS) + KINDS.index((kind, way))
        index = {"n": 0, "s": 1, "e": 2, "w": 3}[way]
        if kind == "slot":
            src, dst = slot_send.at[step, index], slot_recv.at[step, index]
        elif kind == "key":
            src, dst = key_send.at[step, min(index, 2)], key_recv.at[step, index]
        elif kind == "bulk":
            src, dst = bulk_send.at[step, min(index, 2)], bulk_recv.at[step, index]
        else:
            src, dst = back_send.at[step, index], back_recv.at[step, index]
        return pltpu.make_async_remote_copy(
            src_ref=src, dst_ref=dst, send_sem=ssem.at[place], recv_sem=rsem.at[place],
            device_id=at[way], device_id_type=MESH,
        )

    n_far = n_col // GROUP
    far_block = col // GROUP
    member = lax.rem(col, GROUP)

    def lanes_of(i):
        return pl.ds(pl.multiple_of(i * 128, 128), 128)

    def key_copy(step, i, sender):
        return pltpu.make_async_remote_copy(
            src_ref=kf_send.at[step], dst_ref=kf_all.at[step, :, lanes_of(sender)],
            send_sem=fs_sem.at[step, i], recv_sem=fr_sem.at[step, sender],
            device_id=(row, peer(i)), device_id_type=MESH,
        )

    def key_fold(step, act, receiving=False):
        def one(i, carry):
            act(key_copy(step, i, peer(i) if receiving else col))
            return carry

        lax.fori_loop(1, n_col, one, 0)

    def far_copy(step, i, sender):
        return pltpu.make_async_remote_copy(
            src_ref=line_send.at[step], dst_ref=lines.at[step, :, lanes_of(sender)],
            send_sem=far_s.at[step, i], recv_sem=far_r.at[step, sender],
            device_id=(row, peer(i * GROUP)), device_id_type=MESH,
        )

    def near_copy(step, i, sender):
        other = far_block * GROUP + lax.rem(member + i, GROUP)
        return pltpu.make_async_remote_copy(
            src_ref=chosen_send.at[step, i], dst_ref=chosen_all.at[step, sender],
            send_sem=near_s.at[step, i], recv_sem=near_r.at[step, sender],
            device_id=(row, other), device_id_type=MESH,
        )

    near_part = member

    def index_copy(i, sender):
        other = far_block * GROUP + lax.rem(member + i, GROUP)
        return pltpu.make_async_remote_copy(
            src_ref=index_send, dst_ref=index_all.at[sender],
            send_sem=index_s.at[i], recv_sem=index_r.at[sender],
            device_id=(row, other), device_id_type=MESH,
        )

    for i in early:
        loads[i].wait()
    heading = (iota((NDIR, 128), 0).astype(f32) + 0.5) * (2.0 * math.pi / NDIR)
    cos_s[0] = jnp.cos(heading)
    cos_s[1] = jnp.sin(heading)
    windbuf[...] = jnp.zeros_like(windbuf)
    curbuf[...] = jnp.zeros_like(curbuf)
    for y in range(4):
        lanes = slice(y * 128, (y + 1) * 128)
        for i in range(2):
            windbuf[i : i + 1, lanes] = wind_ref[i, y : y + 1, :]
        for i in range(3):
            curbuf[i : i + 1, lanes] = cur_ref[i, y : y + 1, :]
        wet = jnp.broadcast_to(wwet_ref[y : y + 1, :].astype(f32), (8, 128))
        wwet8[:, lanes] = jnp.where(iota((8, 128), 0) < 2, 1.0, wet)

    def speeds():
        rel_x = windbuf[0:1, :] - curbuf[0:1, :]
        rel_y = windbuf[1:2, :] - curbuf[1:2, :]
        for y in range(4):
            lanes = slice(y * 128, (y + 1) * 128)
            relative = rel_x[:, lanes] * cos_s[0] + rel_y[:, lanes] * cos_s[1]
            speed[:, lanes] = jnp.maximum(relative, 0.0) + jnp.log(1.0 + jnp.exp(-jnp.abs(relative)))

    speeds()

    def one_hot(send_ref, cells):
        idxbuf[...] = jnp.full(idxbuf.shape, -1, jnp.int32)
        for j in range(3):
            idxbuf[0:1, j * 128 : j * 128 + SLOT] = send_ref[j]
        hot = iota((cells, 3 * 128), 0) == idxbuf[0:1, :]
        return jnp.where(hot, 1.0, 0.0).astype(bf16)

    whot[...] = one_hot(wsend_ref, 512)

    maps16[0:2, :] = stress_ref[...]
    maps16[2:8, :] = stokes_ref[...]
    maps16[8:10, :] = stress_ref[...]
    maps16[10:16, :] = stokes_ref[...]
    place = iota((16, SPEC), 1)
    freq = ((place.astype(f32) + 0.5) * (1.0 / NDIR)).astype(jnp.int32)
    direction = place - freq * NDIR
    rate_wide = jnp.zeros((16, SPEC), f32)
    gain_wide = jnp.zeros((16, SPEC), f32)
    for f in range(NFREQ):
        rate_wide = jnp.where(freq == f, rate_ref[0, f], rate_wide)
        gain_wide = jnp.where(freq == f, gain_ref[0, f], gain_wide)
    row16 = iota((16, SPEC), 0)
    half = jnp.where(row16 >= 8, 1, 0)
    maps = maps16[...]
    rated = maps * rate_wide
    for pair in range(12):
        high, low = split2(jnp.where(direction == 2 * pair + half, rated, 0.0))
        mall[pair * 16 : pair * 16 + 16, :] = high
        mall[208 + pair * 16 : 208 + pair * 16 + 16, :] = low

    loads[0].wait()
    wide[...] = spec_v[...].astype(f32)
    for y in range(4):
        energy[0, :, y * 128 : (y + 1) * 128] = wide[pl.ds(y, SPEC, stride=4), :].astype(bf16)

    loads[4].wait()
    inter = inter_v[...]
    first = maps.astype(bf16)
    rest = maps - first.astype(f32)
    second = rest.astype(bf16)
    third = (rest - second.astype(f32)).astype(bf16)
    moved = (
        jnp.dot(first, inter, preferred_element_type=f32)
        + jnp.dot(second, inter, preferred_element_type=f32)
        + jnp.dot(third, inter, preferred_element_type=f32)
    )
    last_pair = jnp.where(row16 < 8, maps + moved, maps * gain_wide)
    last_pair = jnp.where((row16 < 2) | ((row16 >= 8) & (row16 < 10)), 0.0, last_pair)
    high, low = split2(last_pair)
    mall[192:208, :] = high
    mall[400:416, :] = low

    def project(step):
        both = jnp.dot(mall[...], energy[step], preferred_element_type=f32)
        proj[...] = both[0:208] + both[208:416]

    def send_slots(step):
        total = proj[192:200, :] + curbuf[2:3, :] * proj[200:208, :]
        for k in range(NDIR):
            total = total + speed[k : k + 1, :] * proj[8 * k : 8 * k + 8, :]
        fields = (total * wwet8[...]).astype(bf16)
        slots = jnp.dot(fields, whot[...], preferred_element_type=f32)
        slot_send[step, 1] = slots[:, 0:128]
        slot_send[step, 0] = slots[:, 256:384]
        return slots[:, 128 : 128 + SLOT].astype(bf16)

    project(0)
    own_slots = send_slots(0)

    @pl.when(jnp.logical_not(top | bottom))
    def _():
        pl.semaphore_wait(barrier, 4)

    @pl.when(bottom)
    def _():
        pl.semaphore_wait(barrier, 3)

    @pl.when(top)
    def _():
        pl.semaphore_wait(barrier, n_col)

    def each(msgs, act, receiving):
        for way, copy in msgs:
            edge = {"n": bottom if receiving else top, "s": top if receiving else bottom}.get(way)
            if edge is None:
                act(copy)
            else:
                pl.when(jnp.logical_not(edge))(lambda copy=copy: act(copy))

    def start(step, kind):
        sent = [(way, message(step, kind, way)) for k, way in KINDS if k == kind]
        each(sent, lambda copy: copy.start(), False)
        return sent

    def wait_for(msgs):
        each(msgs, lambda copy: copy.wait_recv(), True)

    pending = []
    slot_msgs = start(0, "slot")
    pending += slot_msgs

    @pl.when(top)
    def _():
        loads[17].wait()
        index_send[...] = jnp.broadcast_to(fold_ref[...].astype(f32), (8, 128))
        index_all[member] = index_send[...]
        for i in range(1, GROUP):
            index_copy(i, member).start()

    @pl.when(jnp.logical_not(top))
    def _():
        loads[17].wait()

    for i in (10, 11, 12, 13, 14, 15, 16, 20):
        loads[i].wait()
    for y in range(8):
        lanes = slice(y * 128, (y + 1) * 128)
        wet = owet_ref[y : y + 1, :].astype(f32)
        orow[0:1, lanes] = wet
        wet8 = jnp.broadcast_to(wet, (8, 128))
        cor8 = jnp.broadcast_to(cor_ref[y : y + 1, :], (8, 128))
        fw[:, lanes] = jnp.where(iota((8, 128), 0) < 2, wet8, wet8 * cor8)
        backv[:, lanes] = jnp.broadcast_to(eta_ref[y : y + 1, :], (8, 128))
    rows_s[...] = jnp.zeros_like(rows_s)
    rows_s[0:1, 0:LEV] = mix_ref[0:1, :]
    rows_s[1:2, 0:LEV] = tau_ref[...]
    rows_s[2:5, 0:LEV] = sprof_ref[...]
    rows_s[5:6, 0:LEV] = thick_ref[...]
    mixp[...] = jnp.zeros_like(mixp)
    mixp[0:LEV, 0:LEV] = mix_ref[...]

    def wide_row(i):
        return jnp.broadcast_to(rows_s[i : i + 1, :], (8, 128))

    r8 = iota((8, 128), 0)
    lane8 = iota((8, 128), 1)
    along_u = jnp.where(r8 == 0, wide_row(1), 0.0)
    along_v = jnp.where(r8 == 1, wide_row(1), 0.0)
    for b in range(NBAND):
        along_u = jnp.where(r8 == 3 + 2 * b, wide_row(2 + b), along_u)
        along_v = jnp.where(r8 == 2 + 2 * b, -wide_row(2 + b), along_v)
    tpose[...] = jnp.zeros_like(tpose)
    tpose[0:8, :] = along_u
    tpose[8:16, :] = along_v
    turned = jnp.transpose(tpose[...])
    gain_u = turned[0:32, 0:8]
    gain_v = turned[0:32, 8:16]
    m0, thick = wide_row(0), wide_row(5)
    for i, (profile, weight) in enumerate(((along_u, m0), (along_v, m0), (along_u, thick), (along_v, thick))):
        coef[i] = jnp.broadcast_to(jnp.sum(profile * weight, axis=1, keepdims=True), (8, 128))
    m0_far = pltpu.roll(m0, 32, 1)
    thick_far = pltpu.roll(thick, 32, 1)
    kmat[...] = jnp.where(
        r8 == 0, m0, jnp.where(r8 == 1, m0_far, jnp.where(r8 == 2, thick, jnp.where(r8 == 3, thick_far, 0.0)))
    )

    cell = iota((1024, 128), 0)
    spot = iota((1024, 128), 1)
    edge = jnp.where(spot < 8, spot * 128 + 127, jnp.where(spot < 16, (spot - 8) * 128, -1))
    sel[...] = jnp.where(cell == edge, 1.0, 0.0).astype(bf16)
    cell_t = iota((128, 1024), 1)
    spot_t = iota((128, 1024), 0)
    edge_t = jnp.where(spot_t < 8, spot_t * 128, jnp.where(spot_t < 16, (spot_t - 8) * 128 + 127, -1))
    ins[...] = jnp.where(cell_t == edge_t, 1.0, 0.0).astype(bf16)

    ohot[...] = one_hot(osend_ref, 1024)

    @pl.when(top)
    def _():
        hot = iota((n_col * 128, 128), 0) == fold_ref[...]
        fhot[...] = jnp.where(hot, 1.0, 0.0).astype(bf16)

    def prepare_ocean(step):
        kv[...] = jnp.dot(kmat[:, 0:64], vw[...], precision=highest, preferred_element_type=f32)

    loads[9].wait()
    vw[...] = jnp.zeros_like(vw)
    for c in range(2):
        for y in range(8):
            lanes = slice(y * 128, (y + 1) * 128)
            level = vel_v[pl.ds(c * 8 * LEV + y, LEV, stride=8), :]
            vw[c * 32 : c * 32 + LEV, lanes] = level * orow[0:1, lanes]
    prepare_ocean(0)

    def next_transfer(step):
        transfer[...] = jnp.dot(inter_v[...], energy[step], preferred_element_type=f32)

    def update_energy(step):
        level = curbuf[2:3, :]
        wet = wwet8[2:3, :]
        for pair in range(13):
            count = 2 if pair < 12 else 1
            rows = slice(pair * 48, pair * 48 + 24 * count)
            old = energy[step, rows, :].astype(f32)
            parts = []
            for part in range(count):
                f = 2 * pair + part
                e = old[part * 24 : part * 24 + 24]
                t = transfer[f * 24 : f * 24 + 24, :]
                factor = rate_ref[0, f] * speed[...] + gain_ref[0, f] * level
                parts.append(wet * (e + factor * e + t))
            new = parts[0] if count == 1 else jnp.concatenate(parts, axis=0)
            if step == STEPS - 1:
                base, size = pair * 192, 96 * count
                for y in range(4):
                    wide[pl.ds(base + y, 24 * count, stride=4), :] = new[:, y * 128 : (y + 1) * 128]
                spec_out[base : base + size, :] = wide[base : base + size, :].astype(bf16)
            else:
                energy[step + 1, rows, :] = new.astype(bf16)

    next_transfer(0)
    update_energy(0)
    loads[19].wait()
    loads[21].wait()

    def pass_north(step, own_slots, slot_msgs):
        wait_for(slot_msgs)
        from_south = jnp.where(bottom, 0.0, slot_recv[step, 0][:, 0:SLOT]).astype(bf16)
        from_north = jnp.where(top, 0.0, slot_recv[step, 1][:, 0:SLOT]).astype(bf16)
        force = (
            jnp.dot(from_north, orecv_v[0:64, :], preferred_element_type=f32)
            + jnp.dot(own_slots, orecv_v[64:128, :], preferred_element_type=f32)
            + jnp.dot(from_south, orecv_v[128:192, :], preferred_element_type=f32)
        )
        force = force * fw[...]
        forc[...] = force
        for y in range(8):
            lanes = slice(y * 128, (y + 1) * 128)
            tile = force[:, lanes]
            value = kv[:, lanes]
            for i in range(4):
                extra = jnp.sum(tile * coef[i], axis=0, keepdims=True)
                value = value + jnp.where(r8 == i, extra, 0.0)
            keys[y] = value
        key_send[step, 0] = keys[7]
        key_send[step, 1] = keys[0]
        edges = jnp.zeros((8, 128), f32)
        for y in range(8):
            edges = jnp.where(lane8 == y, pltpu.roll(keys[y], y + 1, 1), edges)
            edges = jnp.where(lane8 == 8 + y, pltpu.roll(keys[y], 8 + y, 1), edges)
        key_send[step, 2] = edges
        msgs = start(step, "key")

        @pl.when(top)
        def _():
            line = keys[7].astype(bf16)
            kf_send[step] = line
            kf_all[step, :, lanes_of(col)] = line
            key_fold(step, lambda copy: copy.start())

        force = forc[...]
        for c, gain in enumerate((gain_u, gain_v)):
            forced[c * 32 : c * 32 + 32, :] = vw[c * 32 : c * 32 + 32, :] + jnp.dot(
                gain, force, precision=highest, preferred_element_type=f32
            )
        low = forced[...].astype(bf16)
        bulk_send[step, 0] = low[:, 7 * 128 : 8 * 128]
        bulk_send[step, 1] = low[:, 0:128]
        bulk_send[step, 2] = jnp.dot(low, sel[...], preferred_element_type=f32).astype(bf16)
        bulks = start(step, "bulk")

        @pl.when(top)
        def _():
            line = low[:, 7 * 128 : 8 * 128]
            line_send[step] = line
            lines[step, :, lanes_of(far_block)] = line
            for i in range(1, n_far):
                far_copy(step, i, far_block).start()

        return msgs, bulks

    def select_lines(step):
        @pl.when(top)
        def _():
            if step == 0:
                for i in range(1, GROUP):
                    index_copy(i, lax.rem(member + i, GROUP)).wait_recv()
                spot = iota((n_far * 128, 128), 0)
                column = (spot // 128) * (GROUP * 128) + lax.rem(spot, 128) + member * 128
                for i in range(GROUP):
                    wanted = index_all[lax.rem(member + i, GROUP)][0:1, :].astype(jnp.int32)
                    lhot[i] = jnp.where(column == wanted, 1.0, 0.0).astype(bf16)
            for i in range(1, n_far):
                far_copy(step, i, lax.rem(far_block + i, n_far)).wait_recv()
            for i in range(GROUP):
                chosen = jnp.dot(lines[step], lhot[i], preferred_element_type=f32).astype(bf16)
                if i == 0:
                    chosen_all[step, member] = chosen
                else:
                    chosen_send[step, i] = chosen
                    near_copy(step, i, near_part).start()

    def finish_keys(step, msgs):
        wait_for(msgs)

        @pl.when(top)
        def _():
            key_fold(step, lambda copy: copy.wait_recv(), True)
            key_recv[step, 1] = -jnp.dot(kf_all[step], fhot[...], preferred_element_type=f32)

        south_halo = jnp.where(bottom, 0.0, key_recv[step, 0])
        north_halo = key_recv[step, 1]
        from_west = key_recv[step, 2]
        from_east = key_recv[step, 3]
        backs = []
        for y in range(8):
            lanes = slice(y * 128, (y + 1) * 128)
            here = keys[y]
            up = keys[y + 1] if y < 7 else north_halo
            down = keys[y - 1] if y > 0 else south_halo
            left_in = from_west if y == 0 else pltpu.roll(from_west, 128 - y, 1)
            right_in = pltpu.roll(from_east, 127 - (8 + y), 1)
            left = jnp.where(lane8 == 0, left_in, pltpu.roll(here, 1, 1))
            right = jnp.where(lane8 == 127, right_in, pltpu.roll(here, 127, 1))
            wet = jnp.broadcast_to(orow[0:1, lanes], (8, 128))
            level = here + viscous * (up + down + left + right - 4.0 * here)
            spread = 0.5 * (right - left) + 0.5 * pltpu.roll(up - down, 7, 0)
            elevation = backv[:, lanes] - surface_rate * spread
            value = wet * jnp.where(r8 < 2, level, jnp.where(r8 == 2, elevation, 0.0))
            backv[:, lanes] = value
            if step == STEPS - 1:
                eta_out[y : y + 1, :] = value[2:3, :]
        slots = jnp.dot(backv[...].astype(bf16), ohot[...], preferred_element_type=f32)
        back_send[step, 1] = slots[:, 0:128]
        back_send[step, 0] = slots[:, 256:384]
        own = slots[:, 128 : 128 + SLOT].astype(bf16)
        return own, start(step, "back")

    def finish_current(step, own, msgs):
        wait_for(msgs)
        from_south = jnp.where(bottom, 0.0, back_recv[step, 0][:, 0:SLOT]).astype(bf16)
        from_north = jnp.where(top, 0.0, back_recv[step, 1][:, 0:SLOT]).astype(bf16)
        curbuf[...] = (
            jnp.dot(from_north, wrecv_v[0:64, :], preferred_element_type=f32)
            + jnp.dot(own, wrecv_v[64:128, :], preferred_element_type=f32)
            + jnp.dot(from_south, wrecv_v[128:192, :], preferred_element_type=f32)
        )

    def finish_velocity(step, bulks):
        wait_for(bulks)

        @pl.when(top)
        def _():
            for i in range(1, GROUP):
                near_copy(step, i, lax.rem(member + i, GROUP)).wait_recv()
            total = chosen_all[step, 0].astype(f32)
            for i in range(1, GROUP):
                total = total + chosen_all[step, i].astype(f32)
            bulk_recv[step, 1] = (-total).astype(bf16)

        south_halo = jnp.where(bottom, 0.0, bulk_recv[step, 0].astype(f32))
        north_halo = bulk_recv[step, 1].astype(f32)
        lane64 = iota((64, 128), 1)
        sides = jnp.where(lane64 < 8, bulk_recv[step, 2].astype(f32), bulk_recv[step, 3].astype(f32))
        outer = jnp.dot(sides.astype(bf16), ins[...], preferred_element_type=f32)
        for y in range(8):
            lanes = slice(y * 128, (y + 1) * 128)
            here = forced[:, lanes]
            up = forced[:, (y + 1) * 128 : (y + 2) * 128] if y < 7 else north_halo
            down = forced[:, (y - 1) * 128 : y * 128] if y > 0 else south_halo
            left = jnp.where(lane64 == 0, 0.0, pltpu.roll(here, 1, 1))
            right = jnp.where(lane64 == 127, 0.0, pltpu.roll(here, 127, 1))
            around = up + down + left + right + outer[:, lanes] - 4.0 * here
            smooth[:, lanes] = orow[0:1, lanes] * (here + viscous * around)
        for c in range(2):
            new = jnp.dot(
                mixp[...], smooth[c * 32 : c * 32 + 32, :], precision=highest, preferred_element_type=f32
            )
            if step == STEPS - 1:
                for y in range(8):
                    vel_out[pl.ds(c * 8 * LEV + y, LEV, stride=8), :] = new[0:LEV, y * 128 : (y + 1) * 128]
            else:
                vw[c * 32 : c * 32 + 32, :] = new * orow[0:1, :]

    for step in range(STEPS):
        keys_sent, bulks = pass_north(step, own_slots, slot_msgs)
        pending += keys_sent + bulks
        if step == 0:
            project(1)
        else:
            update_energy(step)
        own_back, backs = finish_keys(step, keys_sent)
        pending += backs
        select_lines(step)
        if step == 0:
            next_transfer(1)
        else:
            pl.when(jnp.logical_not(top))(lambda: finish_velocity(step, bulks))
        finish_current(step, own_back, backs)
        if step == 0:
            speeds()
            own_slots = send_slots(1)
            slot_msgs = start(1, "slot")
            pending += slot_msgs
            finish_velocity(step, bulks)
            prepare_ocean(1)
    for y in range(4):
        for i in range(3):
            cur_out[i, y : y + 1, :] = curbuf[i : i + 1, y * 128 : (y + 1) * 128]
    pl.when(top)(lambda: finish_velocity(STEPS - 1, bulks))
    each(pending, lambda copy: copy.wait_send(), False)

    @pl.when(top)
    def _():
        for step in range(STEPS):
            key_fold(step, lambda copy: copy.wait_send())
            for i in range(1, n_far):
                far_copy(step, i, far_block).wait_send()
            for i in range(1, GROUP):
                near_copy(step, i, near_part).wait_send()
        for i in range(1, GROUP):
            index_copy(i, member).wait_send()


def shards(
    spectra, wind, wave_current, wave_wet, interaction, input_rate, eta_gain, stress_map, stokes_map,
    ocean_vel, ocean_eta, ocean_wet, coriolis, tau_profile, stokes_profile, thickness, mix_inverse,
    fold_index, wave_send, ocean_recv, ocean_send, wave_recv,
):
    n_col = lax.axis_size("col")
    n_far = n_col // GROUP
    vmem = pl.BlockSpec(memory_space=pltpu.VMEM)
    hbm = pl.BlockSpec(memory_space=pltpu.HBM)
    V = pltpu.VMEM
    scratch = [
        V((2400, 128), f32), V((STEPS, SPEC, 512), bf16), V((SPEC, 512), f32), V((16, SPEC), f32),
        V((416, SPEC), bf16), V((208, 512), f32), V((NDIR, 512), f32), V((2, NDIR, 128), f32),
        V((8, 512), f32), V((8, 512), f32), V((8, 512), f32),
        V((512, 384), bf16), V((1024, 384), bf16), V((1, 384), jnp.int32), V((n_col * 128, 128), bf16),
        V((8, 128), f32), V((128, 128), f32), V((32, 32), f32), V((8, 128), f32), V((4, 8, 128), f32),
        V((1, 1024), f32), V((8, 1024), f32), V((64, 1024), f32), V((8, 1024), f32), V((8, 1024), f32),
        V((8, 8, 128), f32), V((8, 1024), f32), V((64, 1024), f32), V((64, 1024), f32),
        V((1024, 128), bf16), V((128, 1024), bf16),
        V((STEPS, 2, 8, 128), f32), V((STEPS, 2, 8, 128), f32),
        V((STEPS, 3, 8, 128), f32), V((STEPS, 4, 8, 128), f32),
        V((STEPS, 3, 64, 128), bf16), V((STEPS, 4, 64, 128), bf16),
        V((STEPS, 2, 8, 128), f32), V((STEPS, 2, 8, 128), f32),
        V((STEPS, 8, 128), bf16), V((STEPS, 8, n_col * 128), bf16),
        V((STEPS, 64, 128), bf16), V((STEPS, 64, n_far * 128), bf16),
        V((STEPS, GROUP, 64, 128), bf16), V((STEPS, GROUP, 64, 128), bf16),
        V((8, 128), f32), V((GROUP, 8, 128), f32), V((GROUP, n_far * 128, 128), bf16),
        pltpu.SemaphoreType.DMA((STEPS * len(KINDS),)), pltpu.SemaphoreType.DMA((STEPS * len(KINDS),)),
        pltpu.SemaphoreType.DMA((STEPS, n_col)), pltpu.SemaphoreType.DMA((STEPS, n_col)),
        pltpu.SemaphoreType.DMA((STEPS, n_far)), pltpu.SemaphoreType.DMA((STEPS, n_far)),
        pltpu.SemaphoreType.DMA((STEPS, GROUP)), pltpu.SemaphoreType.DMA((STEPS, GROUP)),
        pltpu.SemaphoreType.DMA((GROUP,)), pltpu.SemaphoreType.DMA((GROUP,)),
        pltpu.SemaphoreType.DMA((22,)),
    ]
    operands = (
        spectra.reshape(2400, 128), wind, wave_current, wave_wet, interaction,
        input_rate.reshape(1, NFREQ), eta_gain.reshape(1, NFREQ), stress_map, stokes_map,
        ocean_vel.reshape(480, 128), ocean_eta, ocean_wet, coriolis,
        tau_profile.reshape(1, LEV), stokes_profile, thickness.reshape(1, LEV), mix_inverse,
        fold_index.reshape(1, 128),
        wave_send.reshape(3, 1, SLOT), ocean_recv.reshape(192, 1024),
        ocean_send.reshape(3, 1, SLOT), wave_recv.reshape(192, 512),
    )
    held = [(pltpu.SMEM if i in (5, 6) else V)(x.shape, x.dtype) for i, x in enumerate(operands)]
    spec_out, vel_out, eta_out, cur_out = pl.pallas_call(
        kernel,
        name="coupled",
        out_shape=(
            jax.ShapeDtypeStruct((2400, 128), bf16),
            jax.ShapeDtypeStruct((480, 128), f32),
            jax.ShapeDtypeStruct((8, 128), f32),
            jax.ShapeDtypeStruct((3, 4, 128), f32),
        ),
        in_specs=[hbm] * len(operands),
        out_specs=(vmem, vmem, vmem, vmem),
        scratch_shapes=held + scratch,
        compiler_params=pltpu.CompilerParams(
            collective_id=0, has_side_effects=True, vmem_limit_bytes=40 * 1024 * 1024
        ),
    )(*[pltpu.with_memory_space_constraint(x, pltpu.HBM) for x in operands])
    return (
        spec_out.reshape(SPEC, 4, 128),
        vel_out.reshape(2, LEV, 8, 128),
        eta_out,
        cur_out,
    )


def solution(mesh):
    tiled3 = P(None, "row", "col")
    tiled = P("row", "col")
    in_specs = (
        tiled3, tiled3, tiled3, tiled, P(), P(), P(), P(), P(),
        P(None, None, "row", "col"), tiled, tiled, tiled, P(), P(), P(), P(), P("col"),
        P("row", "col", None, None), P("row", "col", None, None, None),
        P("row", "col", None, None), P("row", "col", None, None, None),
    )
    out_specs = (tiled3, P(None, None, "row", "col"), tiled, tiled3)
    return jax.shard_map(shards, mesh=mesh, in_specs=in_specs, out_specs=out_specs, check_vma=False)
```

```python
import math

import jax
import jax.numpy as jnp
from jax import lax
from jax.experimental import pallas as pl
from jax.experimental.pallas import tpu as pltpu
from jax.sharding import PartitionSpec as P

NDIR = 24
NFREQ = 25
LEV = 30
NBAND = 3
STEPS = 2
SLOT = 64
SPEC = NDIR * NFREQ
GROUP = 4

viscous = 0.2
surface_rate = 0.5
highest = lax.Precision.HIGHEST
MESH = pl.DeviceIdType.MESH
f32 = jnp.float32
bf16 = jnp.bfloat16

KINDS = (
    ("slot", "n"), ("slot", "s"),
    ("key", "n"), ("key", "s"), ("key", "e"), ("key", "w"),
    ("bulk", "n"), ("bulk", "s"), ("bulk", "e"), ("bulk", "w"),
    ("back", "n"), ("back", "s"),
)


def iota(shape, dim):
    return lax.broadcasted_iota(jnp.int32, shape, dim)


def split2(x):
    high = x.astype(bf16)
    low = (x - high.astype(f32)).astype(bf16)
    return high, low


def deliver(*refs):
    copies = [pltpu.make_async_copy(refs[i], refs[4 + i], refs[8].at[i]) for i in range(4)]
    for copy in copies:
        copy.start()
    for copy in copies:
        copy.wait()


def kernel(
    *refs,
):
    inputs, refs = refs[:22], refs[22:]
    spec_out, vel_out, eta_out, cur_out = refs[:4]
    local, refs = refs[4:26], refs[26:]
    (
        spec_v, wind_ref, cur_ref, wwet_ref, inter_v, rate_ref, gain_ref, stress_ref, stokes_ref,
        vel_v, eta_ref, owet_ref, cor_ref, tau_ref, sprof_ref, thick_ref, mix_ref, fold_ref,
        wsend_ref, orecv_v, osend_ref, wrecv_v,
    ) = local
    (
    wide, energy, transfer, maps16, mall, proj, speed, cos_s, windbuf, curbuf, wwet8,
    whot, ohot, idxbuf,
    rows_s, tpose, mixp, kmat, coef, orow, fw, vw, kv, forc, keys, backv, forced, smooth,
    sel, ins,
    slot_send, slot_recv, key_send, key_recv, bulk_send, bulk_recv, back_send, back_recv,
    kf_send, kf_all, kn_send, kn_all, line_send, lines, chosen_send, chosen_all, index_send, index_all, lhot,
    ssem, rsem, fs_sem, fr_sem, ks_sem, kr_sem, far_s, far_r, near_s, near_r, index_s, index_r, lsem,
    ) = refs
    n_row, n_col = lax.axis_size("row"), lax.axis_size("col")
    row, col = lax.axis_index("row"), lax.axis_index("col")
    north = (lax.rem(row + 1, n_row), col)
    south = (lax.rem(row + n_row - 1, n_row), col)
    east = (row, lax.rem(col + 1, n_col))
    west = (row, lax.rem(col + n_col - 1, n_col))
    at = {"n": north, "s": south, "e": east, "w": west}
    top = row == n_row - 1
    bottom = row == 0
    barrier = pltpu.get_barrier_semaphore()
    n_far = n_col // GROUP
    far_block = col // GROUP
    member = lax.rem(col, GROUP)

    def peer(i):
        return lax.rem(col + i, n_col)

    def signal_to(device):
        pl.semaphore_signal(barrier, inc=1, device_id=device, device_id_type=MESH)

    @pl.when(jnp.logical_not(bottom))
    def _():
        signal_to(south)

    @pl.when(jnp.logical_not(top))
    def _():
        signal_to(north)
        signal_to(east)
        signal_to(west)

    @pl.when(top)
    def _():
        for i in range(1, n_far):
            signal_to((row, peer(i * GROUP)))
        for i in range(1, GROUP):
            signal_to((row, far_block * GROUP + lax.rem(member + i, GROUP)))

        @pl.when(member == 0)
        def _():
            signal_to(west)

        @pl.when(member == GROUP - 1)
        def _():
            signal_to(east)

    loads = [pltpu.make_async_copy(src, dst, lsem.at[i]) for i, (src, dst) in enumerate(zip(inputs, local))]
    early = (1, 2, 3, 5, 6, 7, 8, 18)
    for i in early + (0, 4, 10, 11, 12, 13, 14, 15, 16, 17, 20, 9, 19, 21):
        loads[i].start()

    def message(step, kind, way):
        place = step * len(KINDS) + KINDS.index((kind, way))
        index = {"n": 0, "s": 1, "e": 2, "w": 3}[way]
        if kind == "slot":
            src, dst = slot_send.at[step, index], slot_recv.at[step, index]
        elif kind == "key":
            src, dst = key_send.at[step, min(index, 2)], key_recv.at[step, index]
        elif kind == "bulk":
            src, dst = bulk_send.at[step, min(index, 2)], bulk_recv.at[step, index]
        else:
            src, dst = back_send.at[step, index], back_recv.at[step, index]
        return pltpu.make_async_remote_copy(
            src_ref=src, dst_ref=dst, send_sem=ssem.at[place], recv_sem=rsem.at[place],
            device_id=at[way], device_id_type=MESH,
        )


    def lanes_of(i):
        return pl.ds(pl.multiple_of(i * 128, 128), 128)

    def key_far(step, i, sender):
        return pltpu.make_async_remote_copy(
            src_ref=kf_send.at[step], dst_ref=kf_all.at[step, :, lanes_of(sender)],
            send_sem=fs_sem.at[step, i], recv_sem=fr_sem.at[step, sender],
            device_id=(row, peer(i * GROUP)), device_id_type=MESH,
        )

    def key_near(step, i, sender):
        other = far_block * GROUP + lax.rem(member + i, GROUP)
        return pltpu.make_async_remote_copy(
            src_ref=kn_send.at[step, i], dst_ref=kn_all.at[step, sender],
            send_sem=ks_sem.at[step, i], recv_sem=kr_sem.at[step, sender],
            device_id=(row, other), device_id_type=MESH,
        )

    def far_copy(step, i, sender):
        return pltpu.make_async_remote_copy(
            src_ref=line_send.at[step], dst_ref=lines.at[step, :, lanes_of(sender)],
            send_sem=far_s.at[step, i], recv_sem=far_r.at[step, sender],
            device_id=(row, peer(i * GROUP)), device_id_type=MESH,
        )

    def near_copy(step, i, sender):
        other = far_block * GROUP + lax.rem(member + i, GROUP)
        return pltpu.make_async_remote_copy(
            src_ref=chosen_send.at[step, i], dst_ref=chosen_all.at[step, sender],
            send_sem=near_s.at[step, i], recv_sem=near_r.at[step, sender],
            device_id=(row, other), device_id_type=MESH,
        )

    near_part = member

    def index_copy(i, sender):
        other = far_block * GROUP + lax.rem(member + i, GROUP)
        return pltpu.make_async_remote_copy(
            src_ref=index_send, dst_ref=index_all.at[sender],
            send_sem=index_s.at[i], recv_sem=index_r.at[sender],
            device_id=(row, other), device_id_type=MESH,
        )

    for i in early:
        loads[i].wait()
    heading = (iota((NDIR, 128), 0).astype(f32) + 0.5) * (2.0 * math.pi / NDIR)
    cos_s[0] = jnp.cos(heading)
    cos_s[1] = jnp.sin(heading)
    windbuf[...] = jnp.zeros_like(windbuf)
    curbuf[...] = jnp.zeros_like(curbuf)
    for y in range(4):
        lanes = slice(y * 128, (y + 1) * 128)
        for i in range(2):
            windbuf[i : i + 1, lanes] = wind_ref[i, y : y + 1, :]
        for i in range(3):
            curbuf[i : i + 1, lanes] = cur_ref[i, y : y + 1, :]
        wet = jnp.broadcast_to(wwet_ref[y : y + 1, :].astype(f32), (8, 128))
        wwet8[:, lanes] = jnp.where(iota((8, 128), 0) < 2, 1.0, wet)

    def speeds():
        rel_x = windbuf[0:1, :] - curbuf[0:1, :]
        rel_y = windbuf[1:2, :] - curbuf[1:2, :]
        for y in range(4):
            lanes = slice(y * 128, (y + 1) * 128)
            relative = rel_x[:, lanes] * cos_s[0] + rel_y[:, lanes] * cos_s[1]
            speed[:, lanes] = jnp.maximum(relative, 0.0) + jnp.log(1.0 + jnp.exp(-jnp.abs(relative)))

    speeds()

    def one_hot(send_ref, cells):
        idxbuf[...] = jnp.full(idxbuf.shape, -1, jnp.int32)
        for j in range(3):
            idxbuf[0:1, j * 128 : j * 128 + SLOT] = send_ref[j]
        hot = iota((cells, 3 * 128), 0) == idxbuf[0:1, :]
        return jnp.where(hot, 1.0, 0.0).astype(bf16)

    whot[...] = one_hot(wsend_ref, 512)

    maps16[0:2, :] = stress_ref[...]
    maps16[2:8, :] = stokes_ref[...]
    maps16[8:10, :] = stress_ref[...]
    maps16[10:16, :] = stokes_ref[...]
    place = iota((16, SPEC), 1)
    freq = ((place.astype(f32) + 0.5) * (1.0 / NDIR)).astype(jnp.int32)
    direction = place - freq * NDIR
    rate_wide = jnp.zeros((16, SPEC), f32)
    gain_wide = jnp.zeros((16, SPEC), f32)
    for f in range(NFREQ):
        rate_wide = jnp.where(freq == f, rate_ref[0, f], rate_wide)
        gain_wide = jnp.where(freq == f, gain_ref[0, f], gain_wide)
    row16 = iota((16, SPEC), 0)
    half = jnp.where(row16 >= 8, 1, 0)
    maps = maps16[...]
    rated = maps * rate_wide
    for pair in range(12):
        high, low = split2(jnp.where(direction == 2 * pair + half, rated, 0.0))
        mall[pair * 16 : pair * 16 + 16, :] = high
        mall[208 + pair * 16 : 208 + pair * 16 + 16, :] = low

    loads[0].wait()
    wide[...] = spec_v[...].astype(f32)
    for y in range(4):
        energy[0, :, y * 128 : (y + 1) * 128] = wide[pl.ds(y, SPEC, stride=4), :].astype(bf16)

    loads[4].wait()
    inter = inter_v[...]
    first = maps.astype(bf16)
    rest = maps - first.astype(f32)
    second = rest.astype(bf16)
    third = (rest - second.astype(f32)).astype(bf16)
    moved = (
        jnp.dot(first, inter, preferred_element_type=f32)
        + jnp.dot(second, inter, preferred_element_type=f32)
        + jnp.dot(third, inter, preferred_element_type=f32)
    )
    last_pair = jnp.where(row16 < 8, maps + moved, maps * gain_wide)
    last_pair = jnp.where((row16 < 2) | ((row16 >= 8) & (row16 < 10)), 0.0, last_pair)
    high, low = split2(last_pair)
    mall[192:208, :] = high
    mall[400:416, :] = low

    def project(step):
        both = jnp.dot(mall[...], energy[step], preferred_element_type=f32)
        proj[...] = both[0:208] + both[208:416]

    def send_slots(step):
        total = proj[192:200, :] + curbuf[2:3, :] * proj[200:208, :]
        for k in range(NDIR):
            total = total + speed[k : k + 1, :] * proj[8 * k : 8 * k + 8, :]
        fields = (total * wwet8[...]).astype(bf16)
        slots = jnp.dot(fields, whot[...], preferred_element_type=f32)
        slot_send[step, 1] = slots[:, 0:128]
        slot_send[step, 0] = slots[:, 256:384]
        return slots[:, 128 : 128 + SLOT].astype(bf16)

    project(0)
    own_slots = send_slots(0)

    @pl.when(jnp.logical_not(top | bottom))
    def _():
        pl.semaphore_wait(barrier, 4)

    @pl.when(bottom)
    def _():
        pl.semaphore_wait(barrier, 3)

    @pl.when(top & ((member == 0) | (member == GROUP - 1)))
    def _():
        pl.semaphore_wait(barrier, n_far + GROUP)

    @pl.when(top & (member > 0) & (member < GROUP - 1))
    def _():
        pl.semaphore_wait(barrier, n_far + GROUP - 1)

    def each(msgs, act, receiving):
        for way, copy in msgs:
            edge = {"n": bottom if receiving else top, "s": top if receiving else bottom}.get(way)
            if edge is None:
                act(copy)
            else:
                pl.when(jnp.logical_not(edge))(lambda copy=copy: act(copy))

    def start(step, kind):
        sent = [(way, message(step, kind, way)) for k, way in KINDS if k == kind]
        each(sent, lambda copy: copy.start(), False)
        return sent

    def wait_for(msgs):
        each(msgs, lambda copy: copy.wait_recv(), True)

    pending = []
    slot_msgs = start(0, "slot")
    pending += slot_msgs

    @pl.when(top)
    def _():
        loads[17].wait()
        index_send[...] = jnp.broadcast_to(fold_ref[...].astype(f32), (8, 128))
        index_all[member] = index_send[...]
        for i in range(1, GROUP):
            index_copy(i, member).start()

    @pl.when(jnp.logical_not(top))
    def _():
        loads[17].wait()

    for i in (10, 11, 12, 13, 14, 15, 16, 20):
        loads[i].wait()
    for y in range(8):
        lanes = slice(y * 128, (y + 1) * 128)
        wet = owet_ref[y : y + 1, :].astype(f32)
        orow[0:1, lanes] = wet
        wet8 = jnp.broadcast_to(wet, (8, 128))
        cor8 = jnp.broadcast_to(cor_ref[y : y + 1, :], (8, 128))
        fw[:, lanes] = jnp.where(iota((8, 128), 0) < 2, wet8, wet8 * cor8)
        backv[:, lanes] = jnp.broadcast_to(eta_ref[y : y + 1, :], (8, 128))
    rows_s[...] = jnp.zeros_like(rows_s)
    rows_s[0:1, 0:LEV] = mix_ref[0:1, :]
    rows_s[1:2, 0:LEV] = tau_ref[...]
    rows_s[2:5, 0:LEV] = sprof_ref[...]
    rows_s[5:6, 0:LEV] = thick_ref[...]
    mixp[...] = jnp.zeros_like(mixp)
    mixp[0:LEV, 0:LEV] = mix_ref[...]

    def wide_row(i):
        return jnp.broadcast_to(rows_s[i : i + 1, :], (8, 128))

    r8 = iota((8, 128), 0)
    lane8 = iota((8, 128), 1)
    along_u = jnp.where(r8 == 0, wide_row(1), 0.0)
    along_v = jnp.where(r8 == 1, wide_row(1), 0.0)
    for b in range(NBAND):
        along_u = jnp.where(r8 == 3 + 2 * b, wide_row(2 + b), along_u)
        along_v = jnp.where(r8 == 2 + 2 * b, -wide_row(2 + b), along_v)
    tpose[...] = jnp.zeros_like(tpose)
    tpose[0:8, :] = along_u
    tpose[8:16, :] = along_v
    turned = jnp.transpose(tpose[...])
    gain_u = turned[0:32, 0:8]
    gain_v = turned[0:32, 8:16]
    m0, thick = wide_row(0), wide_row(5)
    for i, (profile, weight) in enumerate(((along_u, m0), (along_v, m0), (along_u, thick), (along_v, thick))):
        coef[i] = jnp.broadcast_to(jnp.sum(profile * weight, axis=1, keepdims=True), (8, 128))
    m0_far = pltpu.roll(m0, 32, 1)
    thick_far = pltpu.roll(thick, 32, 1)
    kmat[...] = jnp.where(
        r8 == 0, m0, jnp.where(r8 == 1, m0_far, jnp.where(r8 == 2, thick, jnp.where(r8 == 3, thick_far, 0.0)))
    )

    cell = iota((1024, 128), 0)
    spot = iota((1024, 128), 1)
    edge = jnp.where(spot < 8, spot * 128 + 127, jnp.where(spot < 16, (spot - 8) * 128, -1))
    sel[...] = jnp.where(cell == edge, 1.0, 0.0).astype(bf16)
    cell_t = iota((128, 1024), 1)
    spot_t = iota((128, 1024), 0)
    edge_t = jnp.where(spot_t < 8, spot_t * 128, jnp.where(spot_t < 16, (spot_t - 8) * 128 + 127, -1))
    ins[...] = jnp.where(cell_t == edge_t, 1.0, 0.0).astype(bf16)

    ohot[...] = one_hot(osend_ref, 1024)

    def prepare_ocean(step):
        kv[...] = jnp.dot(kmat[:, 0:64], vw[...], precision=highest, preferred_element_type=f32)

    loads[9].wait()
    vw[...] = jnp.zeros_like(vw)
    for c in range(2):
        for y in range(8):
            lanes = slice(y * 128, (y + 1) * 128)
            level = vel_v[pl.ds(c * 8 * LEV + y, LEV, stride=8), :]
            vw[c * 32 : c * 32 + LEV, lanes] = level * orow[0:1, lanes]
    prepare_ocean(0)

    def next_transfer(step):
        transfer[...] = jnp.dot(inter_v[...], energy[step], preferred_element_type=f32)

    def update_energy(step):
        level = curbuf[2:3, :]
        wet = wwet8[2:3, :]
        for pair in range(13):
            count = 2 if pair < 12 else 1
            rows = slice(pair * 48, pair * 48 + 24 * count)
            old = energy[step, rows, :].astype(f32)
            parts = []
            for part in range(count):
                f = 2 * pair + part
                e = old[part * 24 : part * 24 + 24]
                t = transfer[f * 24 : f * 24 + 24, :]
                factor = rate_ref[0, f] * speed[...] + gain_ref[0, f] * level
                parts.append(wet * (e + factor * e + t))
            new = parts[0] if count == 1 else jnp.concatenate(parts, axis=0)
            if step == STEPS - 1:
                base, size = pair * 192, 96 * count
                for y in range(4):
                    wide[pl.ds(base + y, 24 * count, stride=4), :] = new[:, y * 128 : (y + 1) * 128]
                spec_out[base : base + size, :] = wide[base : base + size, :].astype(bf16)
            else:
                energy[step + 1, rows, :] = new.astype(bf16)

    next_transfer(0)
    update_energy(0)
    loads[19].wait()
    loads[21].wait()

    def pass_north(step, own_slots, slot_msgs):
        wait_for(slot_msgs)
        from_south = jnp.where(bottom, 0.0, slot_recv[step, 0][:, 0:SLOT]).astype(bf16)
        from_north = jnp.where(top, 0.0, slot_recv[step, 1][:, 0:SLOT]).astype(bf16)
        force = (
            jnp.dot(from_north, orecv_v[0:64, :], preferred_element_type=f32)
            + jnp.dot(own_slots, orecv_v[64:128, :], preferred_element_type=f32)
            + jnp.dot(from_south, orecv_v[128:192, :], preferred_element_type=f32)
        )
        force = force * fw[...]
        forc[...] = force
        for y in range(8):
            lanes = slice(y * 128, (y + 1) * 128)
            tile = force[:, lanes]
            value = kv[:, lanes]
            for i in range(4):
                extra = jnp.sum(tile * coef[i], axis=0, keepdims=True)
                value = value + jnp.where(r8 == i, extra, 0.0)
            keys[y] = value
        key_send[step, 0] = keys[7]
        key_send[step, 1] = keys[0]
        edges = jnp.zeros((8, 128), f32)
        for y in range(8):
            edges = jnp.where(lane8 == y, pltpu.roll(keys[y], y + 1, 1), edges)
            edges = jnp.where(lane8 == 8 + y, pltpu.roll(keys[y], 8 + y, 1), edges)
        key_send[step, 2] = edges

        @pl.when(top)
        def _():
            line = keys[7].astype(bf16)
            kf_send[step] = line
            kf_all[step, :, lanes_of(far_block)] = line
            for i in range(1, n_far):
                key_far(step, i, far_block).start()

        msgs = start(step, "key")

        force = forc[...]
        for c, gain in enumerate((gain_u, gain_v)):
            forced[c * 32 : c * 32 + 32, :] = vw[c * 32 : c * 32 + 32, :] + jnp.dot(
                gain, force, precision=highest, preferred_element_type=f32
            )
        low = forced[...].astype(bf16)
        bulk_send[step, 0] = low[:, 7 * 128 : 8 * 128]
        bulk_send[step, 1] = low[:, 0:128]
        bulk_send[step, 2] = jnp.dot(low, sel[...], preferred_element_type=f32).astype(bf16)
        bulks = start(step, "bulk")

        @pl.when(top)
        def _():
            line = low[:, 7 * 128 : 8 * 128]
            line_send[step] = line
            lines[step, :, lanes_of(far_block)] = line
            for i in range(1, n_far):
                far_copy(step, i, far_block).start()
            if step == 0:
                for i in range(1, GROUP):
                    index_copy(i, lax.rem(member + i, GROUP)).wait_recv()
                spot = iota((n_far * 128, 128), 0)
                column = (spot // 128) * (GROUP * 128) + lax.rem(spot, 128) + member * 128
                for i in range(GROUP):
                    wanted = index_all[lax.rem(member + i, GROUP)][0:1, :].astype(jnp.int32)
                    lhot[i] = jnp.where(column == wanted, 1.0, 0.0).astype(bf16)

        return msgs, bulks

    def select_lines(step):
        @pl.when(top)
        def _():
            for i in range(1, n_far):
                far_copy(step, i, lax.rem(far_block + i, n_far)).wait_recv()
            for i in range(GROUP):
                chosen = jnp.dot(lines[step], lhot[i], preferred_element_type=f32).astype(bf16)
                if i == 0:
                    chosen_all[step, member] = chosen
                else:
                    chosen_send[step, i] = chosen
                    near_copy(step, i, near_part).start()

    def finish_keys(step, msgs):

        @pl.when(top)
        def _():
            for i in range(1, n_far):
                key_far(step, i, lax.rem(far_block + i, n_far)).wait_recv()
            for i in list(range(1, GROUP)) + [0]:
                chosen = jnp.dot(kf_all[step], lhot[i], preferred_element_type=f32).astype(bf16)
                if i == 0:
                    kn_all[step, member] = chosen
                else:
                    kn_send[step, i] = chosen
                    key_near(step, i, member).start()

        wait_for(msgs)

        @pl.when(top)
        def _():
            for i in range(1, GROUP):
                key_near(step, i, lax.rem(member + i, GROUP)).wait_recv()
            total = kn_all[step, 0].astype(f32)
            for i in range(1, GROUP):
                total = total + kn_all[step, i].astype(f32)
            key_recv[step, 1] = -total

        south_halo = jnp.where(bottom, 0.0, key_recv[step, 0])
        north_halo = key_recv[step, 1]
        from_west = key_recv[step, 2]
        from_east = key_recv[step, 3]
        backs = []
        for y in range(8):
            lanes = slice(y * 128, (y + 1) * 128)
            here = keys[y]
            up = keys[y + 1] if y < 7 else north_halo
            down = keys[y - 1] if y > 0 else south_halo
            left_in = from_west if y == 0 else pltpu.roll(from_west, 128 - y, 1)
            right_in = pltpu.roll(from_east, 127 - (8 + y), 1)
            left = jnp.where(lane8 == 0, left_in, pltpu.roll(here, 1, 1))
            right = jnp.where(lane8 == 127, right_in, pltpu.roll(here, 127, 1))
            wet = jnp.broadcast_to(orow[0:1, lanes], (8, 128))
            level = here + viscous * (up + down + left + right - 4.0 * here)
            spread = 0.5 * (right - left) + 0.5 * pltpu.roll(up - down, 7, 0)
            elevation = backv[:, lanes] - surface_rate * spread
            value = wet * jnp.where(r8 < 2, level, jnp.where(r8 == 2, elevation, 0.0))
            backv[:, lanes] = value
            if step == STEPS - 1:
                eta_out[y : y + 1, :] = value[2:3, :]
        slots = jnp.dot(backv[...].astype(bf16), ohot[...], preferred_element_type=f32)
        back_send[step, 1] = slots[:, 0:128]
        back_send[step, 0] = slots[:, 256:384]
        own = slots[:, 128 : 128 + SLOT].astype(bf16)
        return own, start(step, "back")

    def finish_current(step, own, msgs):
        wait_for(msgs)
        from_south = jnp.where(bottom, 0.0, back_recv[step, 0][:, 0:SLOT]).astype(bf16)
        from_north = jnp.where(top, 0.0, back_recv[step, 1][:, 0:SLOT]).astype(bf16)
        curbuf[...] = (
            jnp.dot(from_north, wrecv_v[0:64, :], preferred_element_type=f32)
            + jnp.dot(own, wrecv_v[64:128, :], preferred_element_type=f32)
            + jnp.dot(from_south, wrecv_v[128:192, :], preferred_element_type=f32)
        )

    def finish_velocity(step, bulks):
        wait_for(bulks)

        @pl.when(top)
        def _():
            for i in range(1, GROUP):
                near_copy(step, i, lax.rem(member + i, GROUP)).wait_recv()
            total = chosen_all[step, 0].astype(f32)
            for i in range(1, GROUP):
                total = total + chosen_all[step, i].astype(f32)
            bulk_recv[step, 1] = (-total).astype(bf16)

        south_halo = jnp.where(bottom, 0.0, bulk_recv[step, 0].astype(f32))
        north_halo = bulk_recv[step, 1].astype(f32)
        lane64 = iota((64, 128), 1)
        sides = jnp.where(lane64 < 8, bulk_recv[step, 2].astype(f32), bulk_recv[step, 3].astype(f32))
        outer = jnp.dot(sides.astype(bf16), ins[...], preferred_element_type=f32)
        for y in range(8):
            lanes = slice(y * 128, (y + 1) * 128)
            here = forced[:, lanes]
            up = forced[:, (y + 1) * 128 : (y + 2) * 128] if y < 7 else north_halo
            down = forced[:, (y - 1) * 128 : y * 128] if y > 0 else south_halo
            left = jnp.where(lane64 == 0, 0.0, pltpu.roll(here, 1, 1))
            right = jnp.where(lane64 == 127, 0.0, pltpu.roll(here, 127, 1))
            around = up + down + left + right + outer[:, lanes] - 4.0 * here
            smooth[:, lanes] = orow[0:1, lanes] * (here + viscous * around)
        for c in range(2):
            new = jnp.dot(
                mixp[...], smooth[c * 32 : c * 32 + 32, :], precision=highest, preferred_element_type=f32
            )
            if step == STEPS - 1:
                for y in range(8):
                    vel_out[pl.ds(c * 8 * LEV + y, LEV, stride=8), :] = new[0:LEV, y * 128 : (y + 1) * 128]
            else:
                vw[c * 32 : c * 32 + 32, :] = new * orow[0:1, :]

    for step in range(STEPS):
        keys_sent, bulks = pass_north(step, own_slots, slot_msgs)
        pending += keys_sent + bulks
        if step == 0:
            project(1)
        else:
            update_energy(step)
        own_back, backs = finish_keys(step, keys_sent)
        pending += backs
        select_lines(step)
        if step == 0:
            next_transfer(1)
        else:
            pl.when(jnp.logical_not(top))(lambda: finish_velocity(step, bulks))
        finish_current(step, own_back, backs)
        if step == 0:
            speeds()
            own_slots = send_slots(1)
            slot_msgs = start(1, "slot")
            pending += slot_msgs
            finish_velocity(step, bulks)
            prepare_ocean(1)
    for y in range(4):
        for i in range(3):
            cur_out[i, y : y + 1, :] = curbuf[i : i + 1, y * 128 : (y + 1) * 128]
    pl.when(top)(lambda: finish_velocity(STEPS - 1, bulks))
    each(pending, lambda copy: copy.wait_send(), False)

    @pl.when(top)
    def _():
        for step in range(STEPS):
            for i in range(1, n_far):
                key_far(step, i, far_block).wait_send()
                far_copy(step, i, far_block).wait_send()
            for i in range(1, GROUP):
                near_copy(step, i, near_part).wait_send()
                key_near(step, i, member).wait_send()
        for i in range(1, GROUP):
            index_copy(i, member).wait_send()


def shards(
    spectra, wind, wave_current, wave_wet, interaction, input_rate, eta_gain, stress_map, stokes_map,
    ocean_vel, ocean_eta, ocean_wet, coriolis, tau_profile, stokes_profile, thickness, mix_inverse,
    fold_index, wave_send, ocean_recv, ocean_send, wave_recv,
):
    n_col = lax.axis_size("col")
    n_far = n_col // GROUP
    vmem = pl.BlockSpec(memory_space=pltpu.VMEM)
    hbm = pl.BlockSpec(memory_space=pltpu.HBM)
    V = pltpu.VMEM
    scratch = [
        V((2400, 128), f32), V((STEPS, SPEC, 512), bf16), V((SPEC, 512), f32), V((16, SPEC), f32),
        V((416, SPEC), bf16), V((208, 512), f32), V((NDIR, 512), f32), V((2, NDIR, 128), f32),
        V((8, 512), f32), V((8, 512), f32), V((8, 512), f32),
        V((512, 384), bf16), V((1024, 384), bf16), V((1, 384), jnp.int32),
        V((8, 128), f32), V((128, 128), f32), V((32, 32), f32), V((8, 128), f32), V((4, 8, 128), f32),
        V((1, 1024), f32), V((8, 1024), f32), V((64, 1024), f32), V((8, 1024), f32), V((8, 1024), f32),
        V((8, 8, 128), f32), V((8, 1024), f32), V((64, 1024), f32), V((64, 1024), f32),
        V((1024, 128), bf16), V((128, 1024), bf16),
        V((STEPS, 2, 8, 128), f32), V((STEPS, 2, 8, 128), f32),
        V((STEPS, 3, 8, 128), f32), V((STEPS, 4, 8, 128), f32),
        V((STEPS, 3, 64, 128), bf16), V((STEPS, 4, 64, 128), bf16),
        V((STEPS, 2, 8, 128), f32), V((STEPS, 2, 8, 128), f32),
        V((STEPS, 8, 128), bf16), V((STEPS, 8, n_far * 128), bf16),
        V((STEPS, GROUP, 8, 128), bf16), V((STEPS, GROUP, 8, 128), bf16),
        V((STEPS, 64, 128), bf16), V((STEPS, 64, n_far * 128), bf16),
        V((STEPS, GROUP, 64, 128), bf16), V((STEPS, GROUP, 64, 128), bf16),
        V((8, 128), f32), V((GROUP, 8, 128), f32), V((GROUP, n_far * 128, 128), bf16),
        pltpu.SemaphoreType.DMA((STEPS * len(KINDS),)), pltpu.SemaphoreType.DMA((STEPS * len(KINDS),)),
        pltpu.SemaphoreType.DMA((STEPS, n_far)), pltpu.SemaphoreType.DMA((STEPS, n_far)),
        pltpu.SemaphoreType.DMA((STEPS, GROUP)), pltpu.SemaphoreType.DMA((STEPS, GROUP)),
        pltpu.SemaphoreType.DMA((STEPS, n_far)), pltpu.SemaphoreType.DMA((STEPS, n_far)),
        pltpu.SemaphoreType.DMA((STEPS, GROUP)), pltpu.SemaphoreType.DMA((STEPS, GROUP)),
        pltpu.SemaphoreType.DMA((GROUP,)), pltpu.SemaphoreType.DMA((GROUP,)),
        pltpu.SemaphoreType.DMA((22,)),
    ]
    operands = (
        spectra.reshape(2400, 128), wind, wave_current, wave_wet, interaction,
        input_rate.reshape(1, NFREQ), eta_gain.reshape(1, NFREQ), stress_map, stokes_map,
        ocean_vel.reshape(480, 128), ocean_eta, ocean_wet, coriolis,
        tau_profile.reshape(1, LEV), stokes_profile, thickness.reshape(1, LEV), mix_inverse,
        fold_index.reshape(1, 128),
        wave_send.reshape(3, 1, SLOT), ocean_recv.reshape(192, 1024),
        ocean_send.reshape(3, 1, SLOT), wave_recv.reshape(192, 512),
    )
    held = [(pltpu.SMEM if i in (5, 6) else V)(x.shape, x.dtype) for i, x in enumerate(operands)]
    spec_out, vel_out, eta_out, cur_out = pl.pallas_call(
        kernel,
        name="coupled",
        out_shape=(
            jax.ShapeDtypeStruct((2400, 128), bf16),
            jax.ShapeDtypeStruct((480, 128), f32),
            jax.ShapeDtypeStruct((8, 128), f32),
            jax.ShapeDtypeStruct((3, 4, 128), f32),
        ),
        in_specs=[hbm] * len(operands),
        out_specs=(vmem, vmem, vmem, vmem),
        scratch_shapes=held + scratch,
        compiler_params=pltpu.CompilerParams(
            collective_id=0, has_side_effects=True, vmem_limit_bytes=40 * 1024 * 1024
        ),
    )(*[pltpu.with_memory_space_constraint(x, pltpu.HBM) for x in operands])
    done = (spec_out, vel_out, eta_out, cur_out)
    spec_out, vel_out, eta_out, cur_out = pl.pallas_call(
        deliver,
        name="deliver",
        out_shape=tuple(jax.ShapeDtypeStruct(x.shape, x.dtype) for x in done),
        in_specs=[vmem] * 4,
        out_specs=(hbm,) * 4,
        scratch_shapes=[pltpu.SemaphoreType.DMA((4,))],
        compiler_params=pltpu.CompilerParams(vmem_limit_bytes=4 * 1024 * 1024),
    )(*done)
    return (
        spec_out.reshape(SPEC, 4, 128),
        vel_out.reshape(2, LEV, 8, 128),
        eta_out,
        cur_out,
    )


def solution(mesh):
    tiled3 = P(None, "row", "col")
    tiled = P("row", "col")
    in_specs = (
        tiled3, tiled3, tiled3, tiled, P(), P(), P(), P(), P(),
        P(None, None, "row", "col"), tiled, tiled, tiled, P(), P(), P(), P(), P("col"),
        P("row", "col", None, None), P("row", "col", None, None, None),
        P("row", "col", None, None), P("row", "col", None, None, None),
    )
    out_specs = (tiled3, P(None, None, "row", "col"), tiled, tiled3)
    return jax.shard_map(shards, mesh=mesh, in_specs=in_specs, out_specs=out_specs, check_vma=False)
```

```python
import math

import jax
import jax.numpy as jnp
from jax import lax
from jax.experimental import pallas as pl
from jax.experimental.pallas import tpu as pltpu
from jax.sharding import PartitionSpec as P

NDIR = 24
NFREQ = 25
LEV = 30
NBAND = 3
STEPS = 2
SLOT = 64
SPEC = NDIR * NFREQ
GROUP = 4

viscous = 0.2
surface_rate = 0.5
highest = lax.Precision.HIGHEST
MESH = pl.DeviceIdType.MESH
f32 = jnp.float32
bf16 = jnp.bfloat16

KINDS = (
    ("slot", "n"), ("slot", "s"),
    ("more", "n2"), ("more", "s2"), ("more", "e"), ("more", "w"),
    ("more", "ne"), ("more", "nw"), ("more", "se"), ("more", "sw"),
    ("wide", "n"), ("wide", "s"), ("wide", "e"), ("wide", "w"),
    ("mask", "n"), ("mask", "s"), ("mask", "e"), ("mask", "w"),
    ("line", "n"), ("line", "s"), ("line", "e"), ("line", "w"),
    ("key", "n"), ("key", "s"), ("key", "e"), ("key", "w"),
    ("bulk", "n"), ("bulk", "s"), ("bulk", "e"), ("bulk", "w"),
    ("back", "n"), ("back", "s"),
)


def iota(shape, dim):
    return lax.broadcasted_iota(jnp.int32, shape, dim)


def split2(x):
    high = x.astype(bf16)
    low = (x - high.astype(f32)).astype(bf16)
    return high, low


def deliver(*refs):
    copies = [pltpu.make_async_copy(refs[i], refs[4 + i], refs[8].at[i]) for i in range(4)]
    for copy in copies:
        copy.start()
    for copy in copies:
        copy.wait()


def kernel(
    *refs,
):
    inputs, refs = refs[:22], refs[22:]
    spec_out, vel_out, eta_out, cur_out = refs[:4]
    local, refs = refs[4:26], refs[26:]
    (
        spec_v, wind_ref, cur_ref, wwet_ref, inter_v, rate_ref, gain_ref, stress_ref, stokes_ref,
        vel_v, eta_ref, owet_ref, cor_ref, tau_ref, sprof_ref, thick_ref, mix_ref, fold_ref,
        wsend_ref, orecv_v, osend_ref, wrecv_v,
    ) = local
    (
    wide, energy, transfer, maps16, mall, proj, speed, cos_s, windbuf, curbuf, wwet8,
    whot, ohot, idxbuf,
    rows_s, tpose, mixp, kmat, coef, orow, fw, vw, kv, forc, keys, backv, forced, smooth,
    sel, ins,
    slot_send, slot_recv, more_send, more_recv, wide_l, wide_es, wide_e, mask_es, mask_r, line_es, line_r, edge_f,
    key_send, key_recv, bulk_send, bulk_recv, back_send, back_recv,
    kf_send, kf_all, kn_send, kn_all, line_send, lines, chosen_send, chosen_all, index_send, index_all, lhot,
    ssem, rsem, fs_sem, fr_sem, ks_sem, kr_sem, far_s, far_r, near_s, near_r, index_s, index_r, lsem,
    ) = refs
    n_row, n_col = lax.axis_size("row"), lax.axis_size("col")
    row, col = lax.axis_index("row"), lax.axis_index("col")
    north = (lax.rem(row + 1, n_row), col)
    south = (lax.rem(row + n_row - 1, n_row), col)
    east = (row, lax.rem(col + 1, n_col))
    west = (row, lax.rem(col + n_col - 1, n_col))
    up, down = lax.rem(row + 1, n_row), lax.rem(row + n_row - 1, n_row)
    right, left = lax.rem(col + 1, n_col), lax.rem(col + n_col - 1, n_col)
    at = {
        "n": north, "s": south, "e": east, "w": west,
        "ne": (up, right), "nw": (up, left), "se": (down, right), "sw": (down, left),
        "n2": (lax.rem(row + 2, n_row), col), "s2": (lax.rem(row + n_row - 2, n_row), col),
    }
    top = row == n_row - 1
    bottom = row == 0
    near_top, near_bottom = row >= n_row - 2, row <= 1
    barrier = pltpu.get_barrier_semaphore()
    n_far = n_col // GROUP
    far_block = col // GROUP
    member = lax.rem(col, GROUP)

    def peer(i):
        return lax.rem(col + i, n_col)

    def signal_to(device):
        pl.semaphore_signal(barrier, inc=1, device_id=device, device_id_type=MESH)

    @pl.when(jnp.logical_not(bottom))
    def _():
        for way in ("s", "se", "sw"):
            signal_to(at[way])

    @pl.when(jnp.logical_not(near_bottom))
    def _():
        signal_to(at["s2"])

    @pl.when(jnp.logical_not(near_top))
    def _():
        signal_to(at["n2"])

    @pl.when(jnp.logical_not(top))
    def _():
        for way in ("n", "ne", "nw"):
            signal_to(at[way])
        signal_to(east)
        signal_to(west)

    @pl.when(top)
    def _():
        for i in range(1, n_far):
            signal_to((row, peer(i * GROUP)))
        for i in range(1, GROUP):
            signal_to((row, far_block * GROUP + lax.rem(member + i, GROUP)))

        @pl.when(member == 0)
        def _():
            signal_to(west)

        @pl.when(member == GROUP - 1)
        def _():
            signal_to(east)

    loads = [pltpu.make_async_copy(src, dst, lsem.at[i]) for i, (src, dst) in enumerate(zip(inputs, local))]
    early = (1, 2, 3, 5, 6, 7, 8, 18)
    for i in early + (0, 4, 10, 11, 12, 13, 14, 15, 16, 17, 20, 9, 19, 21):
        loads[i].start()

    def message(step, kind, way):
        place = step * len(KINDS) + KINDS.index((kind, way))
        index = {"n": 0, "s": 1, "e": 2, "w": 3, "n2": 4, "s2": 5, "ne": 6, "nw": 7, "se": 8, "sw": 9}[way]
        line = slice(7 * 128, 8 * 128) if way == "n" else slice(0, 128)
        if kind == "slot":
            src, dst = slot_send.at[step, index], slot_recv.at[step, index]
        elif kind == "more":
            part = {"n": 2, "s": 0, "e": 1, "w": 1}[way[0]]
            src, dst = more_send.at[part], more_recv.at[index]
        elif kind == "wide":
            if index < 2:
                src, dst = orecv_v.at[:, line], wide_l.at[index]
            else:
                src, dst = wide_es, wide_e.at[index - 2]
        elif kind == "mask":
            src, dst = fw.at[:, line] if index < 2 else mask_es, mask_r.at[index]
        elif kind == "line":
            src, dst = kv.at[:, line] if index < 2 else line_es, line_r.at[index]
        elif kind == "key":
            src, dst = key_send.at[step, min(index, 2)], key_recv.at[step, index]
        elif kind == "bulk":
            src, dst = bulk_send.at[step, min(index, 2)], bulk_recv.at[step, index]
        else:
            src, dst = back_send.at[step, index], back_recv.at[step, index]
        return pltpu.make_async_remote_copy(
            src_ref=src, dst_ref=dst, send_sem=ssem.at[place], recv_sem=rsem.at[place],
            device_id=at[way], device_id_type=MESH,
        )


    def lanes_of(i):
        return pl.ds(pl.multiple_of(i * 128, 128), 128)

    def key_far(step, i, sender):
        return pltpu.make_async_remote_copy(
            src_ref=kf_send.at[step], dst_ref=kf_all.at[step, :, lanes_of(sender)],
            send_sem=fs_sem.at[step, i], recv_sem=fr_sem.at[step, sender],
            device_id=(row, peer(i * GROUP)), device_id_type=MESH,
        )

    def key_near(step, i, sender):
        other = far_block * GROUP + lax.rem(member + i, GROUP)
        return pltpu.make_async_remote_copy(
            src_ref=kn_send.at[step, i], dst_ref=kn_all.at[step, sender],
            send_sem=ks_sem.at[step, i], recv_sem=kr_sem.at[step, sender],
            device_id=(row, other), device_id_type=MESH,
        )

    def far_copy(step, i, sender):
        return pltpu.make_async_remote_copy(
            src_ref=line_send.at[step], dst_ref=lines.at[step, :, lanes_of(sender)],
            send_sem=far_s.at[step, i], recv_sem=far_r.at[step, sender],
            device_id=(row, peer(i * GROUP)), device_id_type=MESH,
        )

    def near_copy(step, i, sender):
        other = far_block * GROUP + lax.rem(member + i, GROUP)
        return pltpu.make_async_remote_copy(
            src_ref=chosen_send.at[step, i], dst_ref=chosen_all.at[step, sender],
            send_sem=near_s.at[step, i], recv_sem=near_r.at[step, sender],
            device_id=(row, other), device_id_type=MESH,
        )

    near_part = member

    def index_copy(i, sender):
        other = far_block * GROUP + lax.rem(member + i, GROUP)
        return pltpu.make_async_remote_copy(
            src_ref=index_send, dst_ref=index_all.at[sender],
            send_sem=index_s.at[i], recv_sem=index_r.at[sender],
            device_id=(row, other), device_id_type=MESH,
        )

    for i in early:
        loads[i].wait()
    heading = (iota((NDIR, 128), 0).astype(f32) + 0.5) * (2.0 * math.pi / NDIR)
    cos_s[0] = jnp.cos(heading)
    cos_s[1] = jnp.sin(heading)
    windbuf[...] = jnp.zeros_like(windbuf)
    curbuf[...] = jnp.zeros_like(curbuf)
    for y in range(4):
        lanes = slice(y * 128, (y + 1) * 128)
        for i in range(2):
            windbuf[i : i + 1, lanes] = wind_ref[i, y : y + 1, :]
        for i in range(3):
            curbuf[i : i + 1, lanes] = cur_ref[i, y : y + 1, :]
        wet = jnp.broadcast_to(wwet_ref[y : y + 1, :].astype(f32), (8, 128))
        wwet8[:, lanes] = jnp.where(iota((8, 128), 0) < 2, 1.0, wet)

    def speeds():
        rel_x = windbuf[0:1, :] - curbuf[0:1, :]
        rel_y = windbuf[1:2, :] - curbuf[1:2, :]
        for y in range(4):
            lanes = slice(y * 128, (y + 1) * 128)
            relative = rel_x[:, lanes] * cos_s[0] + rel_y[:, lanes] * cos_s[1]
            speed[:, lanes] = jnp.maximum(relative, 0.0) + jnp.log(1.0 + jnp.exp(-jnp.abs(relative)))

    speeds()

    def one_hot(send_ref, cells):
        idxbuf[...] = jnp.full(idxbuf.shape, -1, jnp.int32)
        for j in range(3):
            idxbuf[0:1, j * 128 : j * 128 + SLOT] = send_ref[j]
        hot = iota((cells, 3 * 128), 0) == idxbuf[0:1, :]
        return jnp.where(hot, 1.0, 0.0).astype(bf16)

    whot[...] = one_hot(wsend_ref, 512)

    maps16[0:2, :] = stress_ref[...]
    maps16[2:8, :] = stokes_ref[...]
    maps16[8:10, :] = stress_ref[...]
    maps16[10:16, :] = stokes_ref[...]
    place = iota((16, SPEC), 1)
    freq = ((place.astype(f32) + 0.5) * (1.0 / NDIR)).astype(jnp.int32)
    direction = place - freq * NDIR
    rate_wide = jnp.zeros((16, SPEC), f32)
    gain_wide = jnp.zeros((16, SPEC), f32)
    for f in range(NFREQ):
        rate_wide = jnp.where(freq == f, rate_ref[0, f], rate_wide)
        gain_wide = jnp.where(freq == f, gain_ref[0, f], gain_wide)
    row16 = iota((16, SPEC), 0)
    half = jnp.where(row16 >= 8, 1, 0)
    maps = maps16[...]
    rated = maps * rate_wide
    for pair in range(12):
        high, low = split2(jnp.where(direction == 2 * pair + half, rated, 0.0))
        mall[pair * 16 : pair * 16 + 16, :] = high
        mall[208 + pair * 16 : 208 + pair * 16 + 16, :] = low

    loads[0].wait()
    wide[...] = spec_v[...].astype(f32)
    for y in range(4):
        energy[0, :, y * 128 : (y + 1) * 128] = wide[pl.ds(y, SPEC, stride=4), :].astype(bf16)

    loads[4].wait()
    inter = inter_v[...]
    first = maps.astype(bf16)
    rest = maps - first.astype(f32)
    second = rest.astype(bf16)
    third = (rest - second.astype(f32)).astype(bf16)
    moved = (
        jnp.dot(first, inter, preferred_element_type=f32)
        + jnp.dot(second, inter, preferred_element_type=f32)
        + jnp.dot(third, inter, preferred_element_type=f32)
    )
    last_pair = jnp.where(row16 < 8, maps + moved, maps * gain_wide)
    last_pair = jnp.where((row16 < 2) | ((row16 >= 8) & (row16 < 10)), 0.0, last_pair)
    high, low = split2(last_pair)
    mall[192:208, :] = high
    mall[400:416, :] = low

    def project(step):
        both = jnp.dot(mall[...], energy[step], preferred_element_type=f32)
        proj[...] = both[0:208] + both[208:416]

    def send_slots(step):
        total = proj[192:200, :] + curbuf[2:3, :] * proj[200:208, :]
        for k in range(NDIR):
            total = total + speed[k : k + 1, :] * proj[8 * k : 8 * k + 8, :]
        fields = (total * wwet8[...]).astype(bf16)
        slots = jnp.dot(fields, whot[...], preferred_element_type=f32)
        for index, j in ((1, 0), (0, 2)):
            slot_send[step, index, 0:8] = slots[:, j * 128 : (j + 1) * 128]
            slot_send[step, index, 8:16] = slots[:, 128:256]
        if step == 1:
            for j in range(3):
                more_send[j] = slots[:, j * 128 : (j + 1) * 128]
        return slots[:, 128 : 128 + SLOT].astype(bf16)

    project(0)
    own_slots = send_slots(0)

    is_top = lax.div(row + 1, n_row)
    is_border = lax.div(member + 1, GROUP) + 1 - lax.div(member + GROUP - 1, GROUP)
    partners = (
        3 * (1 - is_top)
        + 3 * lax.div(row + n_row - 1, n_row)
        + (1 - lax.div(row + 2, n_row))
        + lax.div(row + n_row - 2, n_row)
        + 2 * (1 - is_top)
        + is_top * (n_far + GROUP - 2 + is_border)
    )
    pl.semaphore_wait(barrier, partners)

    def each(msgs, act, receiving):
        for way, copy in msgs:
            high, low, high2, low2 = top, bottom, near_top, near_bottom
            if receiving:
                high, low, high2, low2 = bottom, top, near_bottom, near_top
            edge = {"n": high, "s": low, "n2": high2, "s2": low2}.get(way if way[-1] == "2" else way[0])
            if edge is None:
                act(copy)
            else:
                pl.when(jnp.logical_not(edge))(lambda copy=copy: act(copy))

    def start(step, kind):
        sent = [(way, message(step, kind, way)) for k, way in KINDS if k == kind]
        each(sent, lambda copy: copy.start(), False)
        return sent

    def wait_for(msgs):
        each(msgs, lambda copy: copy.wait_recv(), True)

    pending = []
    slot_msgs = start(0, "slot")
    pending += slot_msgs

    @pl.when(top)
    def _():
        loads[17].wait()
        index_send[...] = jnp.broadcast_to(fold_ref[...].astype(f32), (8, 128))
        index_all[member] = index_send[...]
        for i in range(1, GROUP):
            index_copy(i, member).start()

    @pl.when(jnp.logical_not(top))
    def _():
        loads[17].wait()

    for i in (10, 11, 12, 13, 14, 15, 16, 20):
        loads[i].wait()
    for y in range(8):
        lanes = slice(y * 128, (y + 1) * 128)
        wet = owet_ref[y : y + 1, :].astype(f32)
        orow[0:1, lanes] = wet
        wet8 = jnp.broadcast_to(wet, (8, 128))
        cor8 = jnp.broadcast_to(cor_ref[y : y + 1, :], (8, 128))
        fw[:, lanes] = jnp.where(iota((8, 128), 0) < 2, wet8, wet8 * cor8)
        backv[:, lanes] = jnp.broadcast_to(eta_ref[y : y + 1, :], (8, 128))
    rows_s[...] = jnp.zeros_like(rows_s)
    rows_s[0:1, 0:LEV] = mix_ref[0:1, :]
    rows_s[1:2, 0:LEV] = tau_ref[...]
    rows_s[2:5, 0:LEV] = sprof_ref[...]
    rows_s[5:6, 0:LEV] = thick_ref[...]
    mixp[...] = jnp.zeros_like(mixp)
    mixp[0:LEV, 0:LEV] = mix_ref[...]
    mixp[32:64, :] = pltpu.roll(mixp[0:32, :], 32, 1)

    def wide_row(i):
        return jnp.broadcast_to(rows_s[i : i + 1, :], (8, 128))

    r8 = iota((8, 128), 0)
    lane8 = iota((8, 128), 1)
    along_u = jnp.where(r8 == 0, wide_row(1), 0.0)
    along_v = jnp.where(r8 == 1, wide_row(1), 0.0)
    for b in range(NBAND):
        along_u = jnp.where(r8 == 3 + 2 * b, wide_row(2 + b), along_u)
        along_v = jnp.where(r8 == 2 + 2 * b, -wide_row(2 + b), along_v)
    tpose[...] = jnp.zeros_like(tpose)
    tpose[0:8, :] = along_u
    tpose[8:16, :] = along_v
    turned = jnp.transpose(tpose[...])
    gain_u = turned[0:32, 0:8]
    gain_v = turned[0:32, 8:16]
    m0, thick = wide_row(0), wide_row(5)
    m0_far = pltpu.roll(m0, 32, 1)
    thick_far = pltpu.roll(thick, 32, 1)
    base = jnp.where(
        r8 == 0, m0, jnp.where(r8 == 1, m0_far, jnp.where(r8 == 2, thick, jnp.where(r8 == 3, thick_far, 0.0)))
    )
    mixed = jnp.dot(base[:, 0:64], mixp[...], precision=highest, preferred_element_type=f32)
    kmat[...] = jnp.where(r8 < 4, base, pltpu.roll(mixed, 4, 0))
    m0_mix = jnp.broadcast_to(kmat[4:5, :], (8, 128))
    thick_mix = jnp.broadcast_to(kmat[6:7, :], (8, 128))
    for i, weight in enumerate((m0, thick, m0_mix, thick_mix)):
        for c, profile in enumerate((along_u, along_v)):
            coef[2 * i + c] = jnp.broadcast_to(jnp.sum(profile * weight, axis=1, keepdims=True), (8, 128))

    cell = iota((1024, 128), 0)
    spot = iota((1024, 128), 1)
    edge = jnp.where(spot < 8, spot * 128 + 127, jnp.where(spot < 16, (spot - 8) * 128, -1))
    sel[...] = jnp.where(cell == edge, 1.0, 0.0).astype(bf16)
    cell_t = iota((128, 1024), 1)
    spot_t = iota((128, 1024), 0)
    edge_t = jnp.where(spot_t < 8, spot_t * 128, jnp.where(spot_t < 16, (spot_t - 8) * 128 + 127, -1))
    ins[...] = jnp.where(cell_t == edge_t, 1.0, 0.0).astype(bf16)

    ohot[...] = one_hot(osend_ref, 1024)

    def prepare_ocean(step):
        kv[...] = jnp.dot(kmat[:, 0:64], vw[...], precision=highest, preferred_element_type=f32)
        if step == 1:

            @pl.when(top)
            def _():
                added = viscous * orow[0:1, 7 * 128 : 8 * 128] * pltpu.roll(key_recv[0, 1], 4, 0)
                kv[:, 7 * 128 : 8 * 128] = kv[:, 7 * 128 : 8 * 128] + jnp.where(r8 < 4, added, 0.0)

            start_more(1)

    loads[9].wait()
    vw[...] = jnp.zeros_like(vw)
    for c in range(2):
        for y in range(8):
            lanes = slice(y * 128, (y + 1) * 128)
            level = vel_v[pl.ds(c * 8 * LEV + y, LEV, stride=8), :]
            vw[c * 32 : c * 32 + LEV, lanes] = level * orow[0:1, lanes]
    prepare_ocean(0)

    def next_transfer(step):
        transfer[...] = jnp.dot(inter_v[...], energy[step], preferred_element_type=f32)

    def update_energy(step):
        level = curbuf[2:3, :]
        wet = wwet8[2:3, :]
        for pair in range(13):
            count = 2 if pair < 12 else 1
            rows = slice(pair * 48, pair * 48 + 24 * count)
            old = energy[step, rows, :].astype(f32)
            parts = []
            for part in range(count):
                f = 2 * pair + part
                e = old[part * 24 : part * 24 + 24]
                t = transfer[f * 24 : f * 24 + 24, :]
                factor = rate_ref[0, f] * speed[...] + gain_ref[0, f] * level
                parts.append(wet * (e + factor * e + t))
            new = parts[0] if count == 1 else jnp.concatenate(parts, axis=0)
            if step == STEPS - 1:
                base, size = pair * 192, 96 * count
                for y in range(4):
                    wide[pl.ds(base + y, 24 * count, stride=4), :] = new[:, y * 128 : (y + 1) * 128]
                spec_out[base : base + size, :] = wide[base : base + size, :].astype(bf16)
            else:
                energy[step + 1, rows, :] = new.astype(bf16)

    next_transfer(0)
    update_energy(0)
    loads[19].wait()
    loads[21].wait()
    def side_columns(tiles):
        edges = jnp.zeros((8, 128), f32)
        for y in range(8):
            edges = jnp.where(lane8 == y, pltpu.roll(tiles[y], y + 1, 1), edges)
            edges = jnp.where(lane8 == 8 + y, pltpu.roll(tiles[y], 8 + y, 1), edges)
        return edges

    fixed_msgs, line_msgs = [], []

    def start_fixed():
        spot16, cell16 = iota((16, 1024), 0), iota((16, 1024), 1)
        edge16 = jnp.where(spot16 < 8, spot16 * 128 + 127, (spot16 - 8) * 128)
        pick = jnp.where(cell16 == edge16, 1.0, 0.0).astype(bf16)
        wide_es[...] = lax.dot_general(
            pick, orecv_v[...], (((1,), (1,)), ((), ())), preferred_element_type=f32
        ).astype(bf16)
        mask_es[...] = side_columns([fw[:, y * 128 : (y + 1) * 128] for y in range(8)])
        fixed_msgs.extend(start(0, "mask") + start(0, "wide"))

    def start_more(step):
        line_es[...] = side_columns([kv[:, y * 128 : (y + 1) * 128] for y in range(8)])
        line_msgs.extend(start(step, "line"))

    def halo_key(force, index):
        force = force * mask_r[index]
        value = line_r[index]
        for i in range(4):
            extra = jnp.sum(force * coef[i], axis=0, keepdims=True)
            value = value + jnp.where(r8 == i, extra, 0.0)
        key_recv[1, index] = value

    def finish_more():
        wait_for(fixed_msgs)
        wait_for(more_msgs)
        wait_for(line_msgs)

        def slots_of(ref, off):
            return jnp.where(off, 0.0, ref[:, 0:SLOT]).astype(bf16)

        def product(parts, weights):
            total = jnp.dot(parts[0], weights[0:64, :], preferred_element_type=f32)
            for j in (1, 2):
                total = total + jnp.dot(parts[j], weights[j * 64 : j * 64 + 64, :], preferred_element_type=f32)
            return total

        own = [more_send[j][:, 0:SLOT].astype(bf16) for j in range(3)]
        south_mid = slots_of(slot_recv.at[1, 0, 8:16], bottom)
        north_mid = slots_of(slot_recv.at[1, 1, 8:16], top)
        halo_key(product((own[0], south_mid, slots_of(more_recv.at[4], near_bottom)), wide_l.at[0]), 0)

        @pl.when(jnp.logical_not(top))
        def _():
            halo_key(product((slots_of(more_recv.at[5], near_top), north_mid, own[2]), wide_l.at[1]), 1)

        for index, high, low in ((2, 8, 6), (3, 9, 7)):
            parts = (
                slots_of(more_recv.at[high], top),
                more_recv[index][:, 0:SLOT].astype(bf16),
                slots_of(more_recv.at[low], bottom),
            )
            total = jnp.zeros((8, 16), f32)
            for j in range(3):
                total = total + lax.dot_general(
                    parts[j], wide_e[index - 2][:, j * 64 : j * 64 + 64], (((1,), (1,)), ((), ())),
                    preferred_element_type=f32,
                )
            edge_f[...] = jnp.zeros_like(edge_f)
            edge_f[:, 0:16] = total
            halo_key(edge_f[...], index)

    def pass_north(step, own_slots, slot_msgs):
        wait_for(slot_msgs)
        from_south = jnp.where(bottom, 0.0, slot_recv[step, 0][0:8, 0:SLOT]).astype(bf16)
        from_north = jnp.where(top, 0.0, slot_recv[step, 1][0:8, 0:SLOT]).astype(bf16)
        force = (
            jnp.dot(from_north, orecv_v[0:64, :], preferred_element_type=f32)
            + jnp.dot(own_slots, orecv_v[64:128, :], preferred_element_type=f32)
            + jnp.dot(from_south, orecv_v[128:192, :], preferred_element_type=f32)
        )
        force = force * fw[...]
        forc[...] = force
        for y in range(8):
            lanes = slice(y * 128, (y + 1) * 128)
            tile = force[:, lanes]
            value = kv[:, lanes]
            for i in range(8 if y == 7 and step == 0 else 4):
                extra = jnp.sum(tile * coef[i], axis=0, keepdims=True)
                value = value + jnp.where(r8 == i, extra, 0.0)
            keys[y] = value

        @pl.when(top)
        def _():
            line = keys[7].astype(bf16)
            kf_send[step] = line
            kf_all[step, :, lanes_of(far_block)] = line
            for i in range(1, n_far):
                key_far(step, i, far_block).start()

        msgs = []
        if step == 0:
            key_send[step, 0] = keys[7]
            key_send[step, 1] = keys[0]
            key_send[step, 2] = side_columns([keys[y] for y in range(8)])
            msgs = start(step, "key")

        if step == 1:
            fold_fix(0)
        force = forc[...]
        for c, gain in enumerate((gain_u, gain_v)):
            forced[c * 32 : c * 32 + 32, :] = vw[c * 32 : c * 32 + 32, :] + jnp.dot(
                gain, force, precision=highest, preferred_element_type=f32
            )
        low = forced[...].astype(bf16)
        bulk_send[step, 0] = low[:, 7 * 128 : 8 * 128]
        bulk_send[step, 1] = low[:, 0:128]
        bulk_send[step, 2] = jnp.dot(low, sel[...], preferred_element_type=f32).astype(bf16)
        bulks = start(step, "bulk")

        @pl.when(top)
        def _():
            line = low[:, 7 * 128 : 8 * 128]
            line_send[step] = line
            lines[step, :, lanes_of(far_block)] = line
            for i in range(1, n_far):
                far_copy(step, i, far_block).start()
            if step == 0:
                for i in range(1, GROUP):
                    index_copy(i, lax.rem(member + i, GROUP)).wait_recv()
                spot = iota((n_far * 128, 128), 0)
                column = (spot // 128) * (GROUP * 128) + lax.rem(spot, 128) + member * 128
                for i in range(GROUP):
                    wanted = index_all[lax.rem(member + i, GROUP)][0:1, :].astype(jnp.int32)
                    lhot[i] = jnp.where(column == wanted, 1.0, 0.0).astype(bf16)

        return msgs, bulks

    def select_lines(step):
        @pl.when(top)
        def _():
            for i in range(1, n_far):
                far_copy(step, i, lax.rem(far_block + i, n_far)).wait_recv()
            for i in range(GROUP):
                chosen = jnp.dot(lines[step], lhot[i], preferred_element_type=f32).astype(bf16)
                if i == 0:
                    chosen_all[step, member] = chosen
                else:
                    chosen_send[step, i] = chosen
                    near_copy(step, i, near_part).start()

    def finish_keys(step, msgs):

        @pl.when(top)
        def _():
            for i in range(1, n_far):
                key_far(step, i, lax.rem(far_block + i, n_far)).wait_recv()
            for i in list(range(1, GROUP)) + [0]:
                chosen = jnp.dot(kf_all[step], lhot[i], preferred_element_type=f32).astype(bf16)
                if i == 0:
                    kn_all[step, member] = chosen
                else:
                    kn_send[step, i] = chosen
                    key_near(step, i, member).start()

        if step == 0:
            wait_for(msgs)
        else:
            finish_more()

        @pl.when(top)
        def _():
            for i in range(1, GROUP):
                key_near(step, i, lax.rem(member + i, GROUP)).wait_recv()
            total = kn_all[step, 0].astype(f32)
            for i in range(1, GROUP):
                total = total + kn_all[step, i].astype(f32)
            key_recv[step, 1] = -total

        south_halo = jnp.where(bottom, 0.0, key_recv[step, 0])
        north_halo = key_recv[step, 1]
        from_west = key_recv[step, 2]
        from_east = key_recv[step, 3]
        backs = []
        for y in range(8):
            lanes = slice(y * 128, (y + 1) * 128)
            here = keys[y]
            up = keys[y + 1] if y < 7 else north_halo
            down = keys[y - 1] if y > 0 else south_halo
            left_in = from_west if y == 0 else pltpu.roll(from_west, 128 - y, 1)
            right_in = pltpu.roll(from_east, 127 - (8 + y), 1)
            left = jnp.where(lane8 == 0, left_in, pltpu.roll(here, 1, 1))
            right = jnp.where(lane8 == 127, right_in, pltpu.roll(here, 127, 1))
            wet = jnp.broadcast_to(orow[0:1, lanes], (8, 128))
            level = here + viscous * (up + down + left + right - 4.0 * here)
            spread = 0.5 * (right - left) + 0.5 * pltpu.roll(up - down, 7, 0)
            elevation = backv[:, lanes] - surface_rate * spread
            value = wet * jnp.where(r8 < 2, level, jnp.where(r8 == 2, elevation, 0.0))
            backv[:, lanes] = value
            if step == STEPS - 1:
                eta_out[y : y + 1, :] = value[2:3, :]
        slots = jnp.dot(backv[...].astype(bf16), ohot[...], preferred_element_type=f32)
        back_send[step, 1] = slots[:, 0:128]
        back_send[step, 0] = slots[:, 256:384]
        own = slots[:, 128 : 128 + SLOT].astype(bf16)
        return own, start(step, "back")

    def finish_current(step, own, msgs):
        wait_for(msgs)
        from_south = jnp.where(bottom, 0.0, back_recv[step, 0][:, 0:SLOT]).astype(bf16)
        from_north = jnp.where(top, 0.0, back_recv[step, 1][:, 0:SLOT]).astype(bf16)
        curbuf[...] = (
            jnp.dot(from_north, wrecv_v[0:64, :], preferred_element_type=f32)
            + jnp.dot(own, wrecv_v[64:128, :], preferred_element_type=f32)
            + jnp.dot(from_south, wrecv_v[128:192, :], preferred_element_type=f32)
        )

    def finish_velocity(step, bulks):
        wait_for(bulks)

        south_halo = jnp.where(bottom, 0.0, bulk_recv[step, 0].astype(f32))
        north_halo = jnp.where(top, 0.0, bulk_recv[step, 1].astype(f32))
        lane64 = iota((64, 128), 1)
        sides = jnp.where(lane64 < 8, bulk_recv[step, 2].astype(f32), bulk_recv[step, 3].astype(f32))
        outer = jnp.dot(sides.astype(bf16), ins[...], preferred_element_type=f32)
        for y in range(8):
            lanes = slice(y * 128, (y + 1) * 128)
            here = forced[:, lanes]
            up = forced[:, (y + 1) * 128 : (y + 2) * 128] if y < 7 else north_halo
            down = forced[:, (y - 1) * 128 : y * 128] if y > 0 else south_halo
            left = jnp.where(lane64 == 0, 0.0, pltpu.roll(here, 1, 1))
            right = jnp.where(lane64 == 127, 0.0, pltpu.roll(here, 127, 1))
            around = up + down + left + right + outer[:, lanes] - 4.0 * here
            smooth[:, lanes] = orow[0:1, lanes] * (here + viscous * around)
        for c in range(2):
            new = jnp.dot(
                mixp[0:32, 0:32], smooth[c * 32 : c * 32 + 32, :], precision=highest, preferred_element_type=f32
            )
            if step == STEPS - 1:
                for y in range(8):
                    vel_out[pl.ds(c * 8 * LEV + y, LEV, stride=8), :] = new[0:LEV, y * 128 : (y + 1) * 128]
            else:
                vw[c * 32 : c * 32 + 32, :] = new * orow[0:1, :]

    def fold_fix(step):
        @pl.when(top)
        def _():
            for i in range(1, GROUP):
                near_copy(step, i, lax.rem(member + i, GROUP)).wait_recv()
            total = chosen_all[step, 0].astype(f32)
            for i in range(1, GROUP):
                total = total + chosen_all[step, i].astype(f32)
            wet = orow[0:1, 7 * 128 : 8 * 128]
            for c in range(2):
                added = jnp.dot(
                    mixp[0:32, 0:32], total[c * 32 : c * 32 + 32], precision=highest, preferred_element_type=f32
                )
                added = -viscous * wet * added
                if step == STEPS - 1:
                    spot = pl.ds(c * 8 * LEV + 7, LEV, stride=8)
                    vel_out[spot, :] = vel_out[spot, :] + added[0:LEV]
                else:
                    rows = slice(c * 32, c * 32 + 32)
                    vw[rows, 7 * 128 : 8 * 128] = vw[rows, 7 * 128 : 8 * 128] + added

    for step in range(STEPS):
        keys_sent, bulks = pass_north(step, own_slots, slot_msgs)
        pending += keys_sent + bulks
        if step == 0:
            start_fixed()
            pending += fixed_msgs
            project(1)
        own_back, backs = finish_keys(step, keys_sent)
        pending += backs
        select_lines(step)
        if step == 0:
            finish_velocity(step, bulks)
            prepare_ocean(1)
            pending += line_msgs
        else:
            update_energy(step)
            finish_velocity(step, bulks)
        finish_current(step, own_back, backs)
        if step == 0:
            speeds()
            own_slots = send_slots(1)
            slot_msgs = start(1, "slot")
            more_msgs = start(1, "more")
            pending += slot_msgs + more_msgs
            next_transfer(1)
    for y in range(4):
        for i in range(3):
            cur_out[i, y : y + 1, :] = curbuf[i : i + 1, y * 128 : (y + 1) * 128]
    fold_fix(STEPS - 1)
    each(pending, lambda copy: copy.wait_send(), False)

    @pl.when(top)
    def _():
        for step in range(STEPS):
            for i in range(1, n_far):
                key_far(step, i, far_block).wait_send()
                far_copy(step, i, far_block).wait_send()
            for i in range(1, GROUP):
                near_copy(step, i, near_part).wait_send()
                key_near(step, i, member).wait_send()
        for i in range(1, GROUP):
            index_copy(i, member).wait_send()


def shards(
    spectra, wind, wave_current, wave_wet, interaction, input_rate, eta_gain, stress_map, stokes_map,
    ocean_vel, ocean_eta, ocean_wet, coriolis, tau_profile, stokes_profile, thickness, mix_inverse,
    fold_index, wave_send, ocean_recv, ocean_send, wave_recv,
):
    n_col = lax.axis_size("col")
    n_far = n_col // GROUP
    vmem = pl.BlockSpec(memory_space=pltpu.VMEM)
    hbm = pl.BlockSpec(memory_space=pltpu.HBM)
    V = pltpu.VMEM
    scratch = [
        V((2400, 128), f32), V((STEPS, SPEC, 512), bf16), V((SPEC, 512), f32), V((16, SPEC), f32),
        V((416, SPEC), bf16), V((208, 512), f32), V((NDIR, 512), f32), V((2, NDIR, 128), f32),
        V((8, 512), f32), V((8, 512), f32), V((8, 512), f32),
        V((512, 384), bf16), V((1024, 384), bf16), V((1, 384), jnp.int32),
        V((8, 128), f32), V((128, 128), f32), V((64, 128), f32), V((8, 128), f32), V((8, 8, 128), f32),
        V((1, 1024), f32), V((8, 1024), f32), V((64, 1024), f32), V((8, 1024), f32), V((8, 1024), f32),
        V((8, 8, 128), f32), V((8, 1024), f32), V((64, 1024), f32), V((64, 1024), f32),
        V((1024, 128), bf16), V((128, 1024), bf16),
        V((STEPS, 2, 16, 128), f32), V((STEPS, 2, 16, 128), f32), V((3, 8, 128), f32), V((10, 8, 128), f32),
        V((2, 192, 128), bf16), V((16, 192), bf16), V((2, 16, 192), bf16), V((8, 128), f32), V((4, 8, 128), f32),
        V((8, 128), f32), V((4, 8, 128), f32), V((8, 128), f32),
        V((STEPS, 3, 8, 128), f32), V((STEPS, 4, 8, 128), f32),
        V((STEPS, 3, 64, 128), bf16), V((STEPS, 4, 64, 128), bf16),
        V((STEPS, 2, 8, 128), f32), V((STEPS, 2, 8, 128), f32),
        V((STEPS, 8, 128), bf16), V((STEPS, 8, n_far * 128), bf16),
        V((STEPS, GROUP, 8, 128), bf16), V((STEPS, GROUP, 8, 128), bf16),
        V((STEPS, 64, 128), bf16), V((STEPS, 64, n_far * 128), bf16),
        V((STEPS, GROUP, 64, 128), bf16), V((STEPS, GROUP, 64, 128), bf16),
        V((8, 128), f32), V((GROUP, 8, 128), f32), V((GROUP, n_far * 128, 128), bf16),
        pltpu.SemaphoreType.DMA((STEPS * len(KINDS),)), pltpu.SemaphoreType.DMA((STEPS * len(KINDS),)),
        pltpu.SemaphoreType.DMA((STEPS, n_far)), pltpu.SemaphoreType.DMA((STEPS, n_far)),
        pltpu.SemaphoreType.DMA((STEPS, GROUP)), pltpu.SemaphoreType.DMA((STEPS, GROUP)),
        pltpu.SemaphoreType.DMA((STEPS, n_far)), pltpu.SemaphoreType.DMA((STEPS, n_far)),
        pltpu.SemaphoreType.DMA((STEPS, GROUP)), pltpu.SemaphoreType.DMA((STEPS, GROUP)),
        pltpu.SemaphoreType.DMA((GROUP,)), pltpu.SemaphoreType.DMA((GROUP,)),
        pltpu.SemaphoreType.DMA((22,)),
    ]
    operands = (
        spectra.reshape(2400, 128), wind, wave_current, wave_wet, interaction,
        input_rate.reshape(1, NFREQ), eta_gain.reshape(1, NFREQ), stress_map, stokes_map,
        ocean_vel.reshape(480, 128), ocean_eta, ocean_wet, coriolis,
        tau_profile.reshape(1, LEV), stokes_profile, thickness.reshape(1, LEV), mix_inverse,
        fold_index.reshape(1, 128),
        wave_send.reshape(3, 1, SLOT), ocean_recv.reshape(192, 1024),
        ocean_send.reshape(3, 1, SLOT), wave_recv.reshape(192, 512),
    )
    held = [(pltpu.SMEM if i in (5, 6) else V)(x.shape, x.dtype) for i, x in enumerate(operands)]
    spec_out, vel_out, eta_out, cur_out = pl.pallas_call(
        kernel,
        name="coupled",
        out_shape=(
            jax.ShapeDtypeStruct((2400, 128), bf16),
            jax.ShapeDtypeStruct((480, 128), f32),
            jax.ShapeDtypeStruct((8, 128), f32),
            jax.ShapeDtypeStruct((3, 4, 128), f32),
        ),
        in_specs=[hbm] * len(operands),
        out_specs=(vmem, vmem, vmem, vmem),
        scratch_shapes=held + scratch,
        compiler_params=pltpu.CompilerParams(
            collective_id=0, has_side_effects=True, vmem_limit_bytes=40 * 1024 * 1024
        ),
    )(*[pltpu.with_memory_space_constraint(x, pltpu.HBM) for x in operands])
    done = (spec_out, vel_out, eta_out, cur_out)
    spec_out, vel_out, eta_out, cur_out = pl.pallas_call(
        deliver,
        name="deliver",
        out_shape=tuple(jax.ShapeDtypeStruct(x.shape, x.dtype) for x in done),
        in_specs=[vmem] * 4,
        out_specs=(hbm,) * 4,
        scratch_shapes=[pltpu.SemaphoreType.DMA((4,))],
        compiler_params=pltpu.CompilerParams(vmem_limit_bytes=4 * 1024 * 1024),
    )(*done)
    return (
        spec_out.reshape(SPEC, 4, 128),
        vel_out.reshape(2, LEV, 8, 128),
        eta_out,
        cur_out,
    )


def solution(mesh):
    tiled3 = P(None, "row", "col")
    tiled = P("row", "col")
    in_specs = (
        tiled3, tiled3, tiled3, tiled, P(), P(), P(), P(), P(),
        P(None, None, "row", "col"), tiled, tiled, tiled, P(), P(), P(), P(), P("col"),
        P("row", "col", None, None), P("row", "col", None, None, None),
        P("row", "col", None, None), P("row", "col", None, None, None),
    )
    out_specs = (tiled3, P(None, None, "row", "col"), tiled, tiled3)
    return jax.shard_map(shards, mesh=mesh, in_specs=in_specs, out_specs=out_specs, check_vma=False)
```
